256 devices in a mesh: az: 16 (over z, core), rg: 16 (over x, y).
Axes of the slice: x: 4, y: 4, z: 8, core: 2. Of those that a mesh axis runs over, the one named last changes fastest.
Arguments:
- raw_echoes: float32 [1024, 4, 2, 8192], P(('az', 'rg')), may hold values from -6 to 6
- chirp_spectrum: float32 [2, 8192], replicated, may hold values from -5 to 5
- reconstruction: float32 [2, 4, 4, 1024], replicated, may hold values from -2 to 2
- delays: int32 [4], replicated, may hold values from 0 to 1023
- azimuth_rate: float32 [8192], P(('az', 'rg')), may hold values from 0.5 to 2
- band_halfwidth: int32 [8192], P(('az', 'rg')), may hold values from 512 to 2048
- migration: int32 [8192], P(('az', 'rg')), may hold values from 8 to 16
Outputs:
- focused_image: float32 [2, 8192, 4096], P(None, ('az', 'rg'))
The draws below stay inside these ranges and needn't reach their ends.
All inputs are finite; a program needn't handle non-finite values.
Results may differ from the reference program's by a relative error of at most 0.00007.
Values sent between devices are 32-bit elements; how exact they have to be, the bound alone decides.
No kernel may reach another device: no remote copies, remote signals or barrier semaphores. Data moves between devices by JAX's collectives and lax.ppermute only.
A program may use at most 64 MiB of HBM per device.

```python
import math
import jax
import jax.numpy as jnp
from jax import lax

NCH = 4
NR = 8192
MIG = 16
PULSES = 1024
DOPPLER = 4096


def set_ends(values, own_key, low, high):
    index_at = [jax.random.randint(jax.random.fold_in(own_key, axis), (), 0, length) for axis, length in enumerate(values.shape)]
    main_axis = values.shape.index(max(values.shape))
    neighbour = index_at[:main_axis] + [(index_at[main_axis] + 1) % values.shape[main_axis]] + index_at[main_axis + 1:]
    return values.at[tuple(index_at)].set(low).at[tuple(neighbour)].set(high)


def levels(own_key, extent, cuts, smallest, top_value):
    def one(axis_at, shards_of):
        steps = jax.random.uniform(jax.random.fold_in(jax.random.fold_in(own_key, 6), axis_at), (shards_of,), jnp.float32, smallest / len(cuts), top_value / len(cuts))
        return jnp.repeat(jnp.exp(steps), extent[axis_at] // shards_of).reshape((-1,) + (1,) * (len(extent) - axis_at - 1))

    factor_of = one(*cuts[0])
    for cut in cuts[1:]:
        factor_of = factor_of * one(*cut)
    return factor_of


def scatter_about(rng, extent, width, most, shards=(), kind=jnp.bfloat16):
    gain = levels(rng, extent, shards, -0.22, 0.18) if shards else 1.0
    values = jax.random.normal(rng, extent, jnp.float32) * width * gain
    return jnp.minimum(jnp.maximum(values, -most), most).astype(kind)


def setup_inputs(seed: int = 0) -> dict:
    splits = jax.random.split(jax.random.key(seed), 8)
    raw_echoes = scatter_about(splits[0], (PULSES, NCH, 2, NR), 1.0, 6.0, ((0, 256),), jnp.float32)
    chirp_spectrum = scatter_about(splits[1], (2, NR), 0.7071, 5.0, (), jnp.float32)
    reconstruction = scatter_about(splits[2], (2, NCH, NCH, PULSES), 0.35, 2.0, (), jnp.float32)
    delays = set_ends(jax.random.randint(splits[3], (NCH,), 0, PULSES), jax.random.fold_in(splits[3], 1), 0, PULSES - 1).astype(jnp.int32)
    azimuth_rate = jnp.clip(jnp.exp(math.log(2.0) - 1.3862944 * jax.random.uniform(splits[4], (NR,), jnp.float32) ** levels(splits[4], (NR,), ((0, 256),), -0.2, 0.2)), 0.5, 2.0)
    band_halfwidth = set_ends(jax.random.randint(splits[5], (NR,), DOPPLER // 8, DOPPLER // 2 + 1), jax.random.fold_in(splits[5], 1), DOPPLER // 8, (DOPPLER // 2 + 1) - 1).astype(jnp.int32)
    migration = set_ends(jax.random.randint(splits[6], (NR,), MIG // 2, MIG + 1), jax.random.fold_in(splits[6], 1), MIG // 2, MIG).astype(jnp.int32)
    return {"raw_echoes": raw_echoes, "chirp_spectrum": chirp_spectrum, "reconstruction": reconstruction, "delays": delays, "azimuth_rate": azimuth_rate, "band_halfwidth": band_halfwidth, "migration": migration}


curvature = 32.0

def reference(raw_echoes, chirp_spectrum, reconstruction, delays, azimuth_rate, band_halfwidth, migration):
    signal = lax.complex(raw_echoes[:, :, 0], raw_echoes[:, :, 1])
    spectrum = jnp.fft.fft(signal, axis=2)
    compressed = jnp.fft.ifft(spectrum * lax.complex(chirp_spectrum[0], -chirp_spectrum[1]), axis=2)
    doppler = jnp.fft.fft(compressed, axis=0) / math.sqrt(PULSES)
    frequency = jnp.arange(PULSES, dtype=jnp.int32)
    angle_turns = frequency[None, :] * delays[:, None] % PULSES
    angles = 2.0 * math.pi / PULSES * angle_turns.astype(jnp.float32)
    alignment = lax.complex(jnp.cos(angles), jnp.sin(angles))
    mixing = lax.complex(reconstruction[0], reconstruction[1]) * alignment[None]
    unfolded = jnp.einsum('bcf,fcr->bfr', mixing, doppler, precision=lax.Precision.HIGHEST)
    unfolded = unfolded.reshape(DOPPLER, NR)
    padded = jnp.pad(unfolded, ((0, 0), (0, MIG)))
    doppler_index = jnp.arange(DOPPLER, dtype=jnp.int32)
    centred = doppler_index - DOPPLER * (doppler_index >= DOPPLER // 2).astype(jnp.int32)
    band_square = band_halfwidth * band_halfwidth
    squared = jnp.minimum((centred * centred)[None, :], band_square[:, None])
    migration_shift = (migration[:, None] * squared + (band_square // 2)[:, None]) // band_square[:, None]
    source_rows = jnp.arange(NR, dtype=jnp.int32)[:, None] + migration_shift
    migrated = jnp.take_along_axis(padded, source_rows.T, axis=1).T
    relative = centred.astype(jnp.float32) / (DOPPLER // 2)
    matched_phase = math.pi * curvature * azimuth_rate[:, None] * (relative * relative)[None, :]
    inside = jnp.abs(centred)[None, :] < band_halfwidth[:, None]
    focused = jnp.where(inside, migrated * lax.complex(jnp.cos(matched_phase), jnp.sin(matched_phase)), 0.0)
    focused_image = jnp.fft.ifft(focused, axis=1) * math.sqrt(DOPPLER)
    return jnp.stack([jnp.real(focused_image), jnp.imag(focused_image)]).astype(jnp.float32)
```

```python
import functools
import math

import jax
import jax.numpy as jnp
import ml_dtypes
import numpy as np
from jax import lax
from jax.experimental import pallas as pl
from jax.experimental.pallas import tpu as pltpu
from jax.sharding import PartitionSpec as P

AXES = ("az", "rg")
F32 = jnp.float32
BF16 = jnp.bfloat16


def split_np(matrix):
    matrix = np.asarray(matrix, np.float64)
    high = matrix.astype(np.float32).astype(ml_dtypes.bfloat16)
    low = (matrix - high.astype(np.float64)).astype(np.float32).astype(ml_dtypes.bfloat16)
    return high, low


def phases(rows, columns, length, sign):
    turns = np.outer(np.asarray(rows), np.asarray(columns)) % length
    angle = sign * 2.0 * np.pi * turns / length
    return np.cos(angle), np.sin(angle)


def complex_left(cosine, sine):
    return np.block([[cosine, -sine], [sine, cosine]])


@functools.lru_cache(None)
def constants():
    out = {}
    c, s = phases(np.arange(64), np.arange(64), 64, -1)
    m = complex_left(c, s).reshape(128, 2, 64).transpose(0, 2, 1).reshape(128, 128)
    h, l = split_np(m)
    out["w1"] = np.concatenate([h, h, l], axis=1)
    order = np.arange(128).reshape(64, 2).T.reshape(-1)
    c, s = phases(np.arange(128), order, 128, -1)
    out["w2h"], out["w2l"] = split_np(np.block([[c, s], [-s, c]]))
    c, s = phases(order, np.arange(128), 128, 1)
    out["w3h"], out["w3l"] = split_np(np.block([[c, s], [-s, c]]))
    c, s = phases(np.arange(64), np.arange(64), 64, 1)
    h, l = split_np(complex_left(c, s) / 8192.0)
    out["w4"] = np.concatenate([h, h, l], axis=1)
    c, s = phases(np.arange(64), np.arange(128), 8192, -1)
    out["t1"] = np.stack([c, s]).astype(np.float32)
    fm = np.arange(256).reshape(16, 4, 4).transpose(2, 1, 0).reshape(-1)
    c, s = phases(fm, np.arange(256), 256, -1)
    out["w5h"], out["w5l"] = split_np(complex_left(c, s) / 32.0)
    grid = fm.reshape(4, 64)
    tables = []
    for pulse in (1, 2, 3):
        angle = -2.0 * np.pi * (pulse * grid % 1024) / 1024
        angle = np.repeat(angle.T, 32, axis=1)
        tables.append(np.stack([np.cos(angle), np.sin(angle)]))
    out["t5"] = np.stack(tables).astype(np.float32)
    c, s = phases(np.arange(256), np.arange(256), 256, 1)
    out["w6h"], out["w6l"] = split_np(np.block([[c, s], [-s, c]]) / 64.0)
    c, s = phases(np.arange(16), np.arange(256), 4096, 1)
    out["t6"] = np.stack([c, s]).astype(np.float32)
    return out


def split(value):
    high = value.astype(BF16)
    return high, (value - high.astype(F32)).astype(BF16)


def dot(a, b):
    return jnp.dot(a, b, preferred_element_type=F32)


def dot3(a, bh, bl):
    ah, al = split(a)
    return dot(ah, bh) + dot(ah, bl) + dot(al, bh)


def block_transpose(v):
    lane = lax.broadcasted_iota(jnp.int32, v[0].shape, 1)
    low64 = lane < 64
    low32 = (lane & 32) == 0
    a = [None] * 4
    for i in (0, 1):
        a[i] = jnp.where(low64, v[i], pltpu.roll(v[i + 2], 64, 1))
        a[i + 2] = jnp.where(low64, pltpu.roll(v[i], 64, 1), v[i + 2])
    o = [None] * 4
    for i in (0, 2):
        o[i] = jnp.where(low32, a[i], pltpu.roll(a[i + 1], 32, 1))
        o[i + 1] = jnp.where(low32, pltpu.roll(a[i], 96, 1), a[i + 1])
    return o


def range_kernel(raw, chirp, w1, w2h, w2l, w3h, w3l, w4, t1, out):
    tr, ti = t1[0], t1[1]
    chirp_parts = []
    for part in (0, 1):
        natural = chirp[pl.ds(part, 64, stride=2), :]
        turned = natural.T
        chirp_parts.append(jnp.concatenate([turned[:64], turned[64:]], axis=1))
    cr, ci = chirp_parts
    for channel in range(4):
        x = jnp.concatenate([raw[pulse * 4 + channel] for pulse in range(4)], axis=1)
        xh, xl = split(x)
        a = dot(w1[...], jnp.concatenate([xh, xl, xh], axis=0))
        rows = []
        for pulse in range(4):
            ar = a[:64, pulse * 128 : pulse * 128 + 128]
            ai = a[64:, pulse * 128 : pulse * 128 + 128]
            rows.append(jnp.concatenate([ar * tr - ai * ti, ar * ti + ai * tr], axis=1))
        b = dot3(jnp.concatenate(rows, axis=0), w2h[...], w2l[...])
        rows = []
        for pulse in range(4):
            br = b[pulse * 64 : pulse * 64 + 64, :128]
            bi = b[pulse * 64 : pulse * 64 + 64, 128:]
            rows.append(jnp.concatenate([br * cr + bi * ci, bi * cr - br * ci], axis=1))
        b = dot3(jnp.concatenate(rows, axis=0), w3h[...], w3l[...])
        columns = []
        for pulse in range(4):
            br = b[pulse * 64 : pulse * 64 + 64, :128]
            bi = b[pulse * 64 : pulse * 64 + 64, 128:]
            columns.append(jnp.concatenate([br * tr + bi * ti, bi * tr - br * ti], axis=0))
        xh, xl = split(jnp.concatenate(columns, axis=1))
        a = dot(w4[...], jnp.concatenate([xh, xl, xh], axis=0))
        for part in (0, 1):
            o = block_transpose(
                [a[part * 64 : part * 64 + 64, p * 128 : p * 128 + 128] for p in range(4)]
            )
            for low in range(4):
                out[pl.ds(low * 8 + channel * 2 + part, 64, stride=32), :] = o[low]


def table_kernel(rate, half, mig, coef, spread, mix, phase, index):
    for entry in range(32):
        mix[entry] = lax.dot_general(
            coef[entry], spread[...], (((0,), (0,)), ((), ())), preferred_element_type=F32
        )
    shape = (16, 128)
    lane = lax.broadcasted_iota(jnp.int32, shape, 1)
    row = lax.broadcasted_iota(jnp.int32, shape, 0)
    bin_index = lane & 31
    width = jnp.broadcast_to(half[0:1, :], shape)
    square = width * width
    half_square = lax.shift_right_logical(square, 1)
    inverse = 1.0 / square.astype(F32)
    moved = jnp.broadcast_to(mig[0:1, :], shape)
    speed = jnp.broadcast_to(rate[0:1, :], shape) * 16.0
    for middle in range(4):
        for block in range(16):
            d = (row + block * 16) * 16 + middle * 4 + lax.shift_right_logical(lane, 5)
            centred = jnp.where(d >= 2048, d - 4096, d)
            c2 = centred * centred
            number = moved * jnp.minimum(c2, square) + half_square
            shift = (number.astype(F32) * inverse).astype(jnp.int32)
            rest = number - shift * square
            shift = shift + jnp.where(rest >= square, 1, 0) - jnp.where(rest < 0, 1, 0)
            source = bin_index + shift
            index[middle, block * 16 : block * 16 + 16, :] = (
                (lane & 96) + (source & 31) + jnp.where(source >= 32, 128, 0)
            )
            turns = speed * (c2.astype(F32) * (1.0 / 4194304.0))
            turns = turns - jnp.floor(turns + 0.5)
            angle = turns * (2.0 * math.pi)
            inside = jnp.abs(centred) < width
            phase[middle, 0, block * 16 : block * 16 + 16, :] = jnp.where(
                inside, jnp.cos(angle), 0.0
            )
            phase[middle, 1, block * 16 : block * 16 + 16, :] = jnp.where(
                inside, jnp.sin(angle), 0.0
            )


def azimuth_kernel(received, mix, w5h, w5l, t5, unfolded, margin, g):
    for pair in range(2):
        columns = []
        for channel in (2 * pair, 2 * pair + 1):
            columns.append(
                jnp.concatenate(
                    [received[pl.ds(channel * 2 + part, 256, stride=8), :] for part in (0, 1)],
                    axis=0,
                )
            )
        zh, zl = split(jnp.concatenate(columns, axis=1))
        g[:, pair * 256 : pair * 256 + 256] = (
            dot(w5h[...], zh) + dot(w5h[...], zl) + dot(w5l[...], zh)
        )
    lane = lax.broadcasted_iota(jnp.int32, (8, 128), 1)
    first = (lane & 16) == 0
    for tile in range(8):
        spectrum = []
        for channel in range(4):
            parts = []
            for part in (0, 1):
                parts.append(
                    block_transpose(
                        [
                            g[
                                part * 256 + low * 64 + tile * 8 : part * 256 + low * 64 + tile * 8 + 8,
                                channel * 128 : channel * 128 + 128,
                            ]
                            for low in range(4)
                        ]
                    )
                )
            xr, xi = [parts[0][0]], [parts[1][0]]
            for pulse in (1, 2, 3):
                tr = t5[pulse - 1, 0, tile * 8 : tile * 8 + 8, :]
                ti = t5[pulse - 1, 1, tile * 8 : tile * 8 + 8, :]
                r, i = parts[0][pulse], parts[1][pulse]
                xr.append(r * tr - i * ti)
                xi.append(r * ti + i * tr)
            ar, ai = xr[0] + xr[2], xi[0] + xi[2]
            br, bi = xr[0] - xr[2], xi[0] - xi[2]
            er, ei = xr[1] + xr[3], xi[1] + xi[3]
            dr, di = xr[1] - xr[3], xi[1] - xi[3]
            spectrum.append(
                [(ar + er, ai + ei), (br + di, bi - dr), (ar - er, ai - ei), (br - di, bi + dr)]
            )
        middle, sub = tile // 2, tile % 2
        for high in range(4):
            kept = []
            for band in range(4):
                real = imag = None
                for channel in range(4):
                    dr, di = spectrum[channel][high]
                    at = high * 64 + tile * 8
                    mr = mix[band * 4 + channel, at : at + 8, :]
                    mi = mix[16 + band * 4 + channel, at : at + 8, :]
                    r = mr * dr - mi * di
                    i = mr * di + mi * dr
                    real = r if real is None else real + r
                    imag = i if imag is None else imag + i
                kept.append((real, imag))
                at = band * 64 + high * 16 + sub * 8
                unfolded[middle, 0, at : at + 8, :] = real
                unfolded[middle, 1, at : at + 8, :] = imag
            for band in (0, 1):
                at = band * 64 + high * 16 + sub * 8
                for part in (0, 1):
                    margin[middle, part, at : at + 8, :] = jnp.where(
                        first, kept[band][part], pltpu.roll(kept[band + 2][part], 16, 1)
                    )


def mul_i(value, quarter):
    r, i = value
    return [(r, i), (-i, r), (-r, -i), (i, -r)][quarter % 4]


def add(a, b):
    return (a[0] + b[0], a[1] + b[1])


def sub(a, b):
    return (a[0] - b[0], a[1] - b[1])


def inverse4(x):
    a, b = add(x[0], x[2]), sub(x[0], x[2])
    e, d = add(x[1], x[3]), mul_i(sub(x[1], x[3]), 1)
    return [add(a, e), add(b, d), sub(a, e), sub(b, d)]


def lanes_taken(value, index):
    return jnp.take_along_axis(value, index, axis=1)


def image_kernel(unfolded, margin, phase, index, w6h, w6l, t6, out, fh, fl, y):
    for middle in range(4):
        for block in range(16):
            at = block * 16
            source = block % 8 * 16
            packed = index[middle, at : at + 16, :]
            beyond = packed >= 128
            lanes = packed & 127
            values = []
            for part in (0, 1):
                own = unfolded[middle, part, at : at + 16, :]
                other = margin[middle, part, source : source + 16, :]
                if block >= 8:
                    other = pltpu.roll(other, 112, 1)
                values.append(
                    jnp.where(beyond, lanes_taken(other, lanes), lanes_taken(own, lanes))
                )
            pr = phase[middle, 0, at : at + 16, :]
            pi = phase[middle, 1, at : at + 16, :]
            for part, value in enumerate(
                (values[0] * pr - values[1] * pi, values[0] * pi + values[1] * pr)
            ):
                high, low = split(value)
                fh[middle, part * 256 + at : part * 256 + at + 16, :] = high
                fl[middle, part * 256 + at : part * 256 + at + 16, :] = low

        def turned(a, b):
            return lax.dot_general(a, b, (((0,), (0,)), ((), ())), preferred_element_type=F32)

        y[middle] = (
            turned(fh[middle], w6h[...])
            + turned(fh[middle], w6l[...])
            + turned(fl[middle], w6h[...])
        )
    for column in range(2):
        for tile in range(4):
            inner = []
            for low in range(4):
                values = []
                for middle in range(4):
                    d1 = middle * 4 + low
                    at = low * 32 + tile * 8
                    r = y[middle, at : at + 8, column * 128 : column * 128 + 128]
                    i = y[middle, at : at + 8, 256 + column * 128 : 256 + column * 128 + 128]
                    if d1:
                        tr = t6[0, d1 : d1 + 1, column * 128 : column * 128 + 128]
                        ti = t6[1, d1 : d1 + 1, column * 128 : column * 128 + 128]
                        r, i = r * tr - i * ti, r * ti + i * tr
                    values.append((r, i))
                inner.append(inverse4(values))
            for qa in range(4):
                values = []
                for low in range(4):
                    v = inner[low][qa]
                    turn = low * qa
                    if turn % 4 == 0:
                        v = mul_i(v, turn // 4)
                    else:
                        c = math.cos(2 * math.pi * turn / 16)
                        s = math.sin(2 * math.pi * turn / 16)
                        v = (v[0] * c - v[1] * s, v[0] * s + v[1] * c)
                    values.append(v)
                for qb, v in enumerate(inverse4(values)):
                    lanes = (qa + 4 * qb) * 256 + column * 128
                    out[0, tile * 8 : tile * 8 + 8, lanes : lanes + 128] = v[0]
                    out[1, tile * 8 : tile * 8 + 8, lanes : lanes + 128] = v[1]


VMEM = pl.BlockSpec(memory_space=pltpu.VMEM)


def call(kernel, out_shape, scratch, limit, flops, *operands):
    multi = isinstance(out_shape, tuple)
    return pl.pallas_call(
        kernel,
        out_shape=out_shape,
        in_specs=[VMEM] * len(operands),
        out_specs=(VMEM,) * len(out_shape) if multi else VMEM,
        scratch_shapes=scratch,
        compiler_params=pltpu.CompilerParams(vmem_limit_bytes=limit),
        cost_estimate=pl.CostEstimate(flops=flops, bytes_accessed=4 << 20, transcendentals=0),
    )(*operands)


def shape(*dims, dtype=F32):
    return jax.ShapeDtypeStruct(dims, dtype)


def mixing_coefficients(reconstruction, delays):
    frequency = jnp.arange(1024, dtype=jnp.int32)
    angles = (
        2.0 * math.pi / 1024 * (frequency[None, :] * delays[:, None] % 1024).astype(F32)
    )
    cosine, sine = jnp.cos(angles)[None], jnp.sin(angles)[None]
    real = reconstruction[0] * cosine - reconstruction[1] * sine
    imag = reconstruction[0] * sine + reconstruction[1] * cosine
    both = jnp.stack([real, imag]).reshape(32, 4, 16, 4, 4)
    return both.transpose(0, 4, 1, 3, 2).reshape(32, 4, 256)


def exact_terms(value):
    terms = []
    for _ in range(3):
        term = lax.reduce_precision(value, 8, 7)
        terms.append(term)
        value = value - term
    return jnp.concatenate(terms, axis=1).astype(BF16)


def local(raw, chirp, reconstruction, delays, rate, half, mig):
    k = constants()
    raw = raw.reshape(16, 2, 64, 128).transpose(0, 2, 1, 3).reshape(16, 128, 128)
    chirp = chirp.reshape(2, 64, 128).transpose(1, 0, 2).reshape(128, 128)
    compressed = call(
        range_kernel, shape(2048, 128), [], 24 << 20, 1 << 30,
        raw, chirp, k["w1"], k["w2h"], k["w2l"], k["w3h"], k["w3l"], k["w4"], k["t1"],
    )
    received = lax.all_to_all(compressed.reshape(256, 8, 128), AXES, 0, 0, tiled=True)
    received = received.reshape(2048, 128)

    def across(value):
        return jnp.broadcast_to(jnp.tile(value, 4)[None], (8, 128))

    coef = exact_terms(mixing_coefficients(reconstruction, delays))
    spread = np.tile(np.repeat(np.eye(4), 32, axis=1), (3, 1)).astype(ml_dtypes.bfloat16)
    mix, phase, index = call(
        table_kernel,
        (shape(32, 256, 128), shape(4, 2, 256, 128), shape(4, 256, 128, dtype=jnp.int32)),
        [], 16 << 20, 1 << 28,
        across(rate), across(half), across(mig), coef, spread,
    )
    unfolded, margin = call(
        azimuth_kernel, (shape(4, 2, 256, 128), shape(4, 2, 128, 128)),
        [pltpu.VMEM((512, 512), F32)], 24 << 20, 1 << 30,
        received, mix, k["w5h"], k["w5l"], k["t5"],
    )
    pairs = [(i, i - 1) for i in range(1, lax.axis_size(AXES))]
    margin = lax.ppermute(margin, AXES, pairs)
    return call(
        image_kernel, shape(2, 32, 4096),
        [
            pltpu.VMEM((4, 512, 128), BF16),
            pltpu.VMEM((4, 512, 128), BF16),
            pltpu.VMEM((4, 128, 512), F32),
        ],
        24 << 20, 1 << 30,
        unfolded, margin, phase, index, k["w6h"], k["w6l"], k["t6"],
    )


def solution(mesh):
    in_specs = (P(AXES, None, None, None), P(), P(), P(), P(AXES), P(AXES), P(AXES))
    return jax.shard_map(
        local, mesh=mesh, in_specs=in_specs, out_specs=P(None, AXES, None), check_vma=False
    )
```

```python
import functools
import math

import jax
import jax.numpy as jnp
import ml_dtypes
import numpy as np
from jax import lax
from jax.experimental import pallas as pl
from jax.experimental.pallas import tpu as pltpu
from jax.sharding import PartitionSpec as P

AXES = ("az", "rg")
GROUPS = 2
EXPAND = 8
COMBINE = 1
F32 = jnp.float32
BF16 = jnp.bfloat16


def split_np(matrix):
    matrix = np.asarray(matrix, np.float64)
    high = matrix.astype(np.float32).astype(ml_dtypes.bfloat16)
    low = (matrix - high.astype(np.float64)).astype(np.float32).astype(ml_dtypes.bfloat16)
    return high, low


def phases(rows, columns, length, sign):
    turns = np.outer(np.asarray(rows), np.asarray(columns)) % length
    angle = sign * 2.0 * np.pi * turns / length
    return np.cos(angle), np.sin(angle)


def complex_left(cosine, sine):
    return np.block([[cosine, -sine], [sine, cosine]])


@functools.lru_cache(None)
def constants():
    out = {}
    c, s = phases(np.arange(64), np.arange(64), 64, -1)
    m = complex_left(c, s).reshape(128, 2, 64).transpose(0, 2, 1).reshape(128, 128)
    h, l = split_np(m)
    first = np.concatenate([h, h, l], axis=1)
    c, s = phases(np.arange(64), np.arange(64), 64, 1)
    h, l = split_np(complex_left(c, s) / 8192.0)
    out["wa"] = np.stack([first, np.concatenate([h, h, l], axis=1)])
    order = np.arange(128).reshape(64, 2).T.reshape(-1)
    c, s = phases(np.arange(128), order, 128, -1)
    pair = split_np(np.block([[c, s], [-s, c]]))
    c, s = phases(order, np.arange(128), 128, 1)
    out["wb"] = np.stack(pair + split_np(np.block([[c, s], [-s, c]])))
    c, s = phases(np.arange(64), np.arange(128), 8192, -1)
    out["t1"] = np.stack([c, s]).astype(np.float32)
    fm = np.arange(256).reshape(16, 4, 4).transpose(2, 1, 0).reshape(-1)
    c, s = phases(fm, np.arange(256), 256, 1)
    out["w5"] = np.stack(split_np(np.concatenate([s, c, -s], axis=0) / 32.0))
    grid = fm.reshape(4, 64)
    tables = []
    for pulse in (1, 2, 3):
        angle = -2.0 * np.pi * (pulse * grid % 1024) / 1024
        angle = np.repeat(angle.T, 32, axis=1)
        tables.append(np.stack([np.cos(angle), np.sin(angle)]))
    out["t5"] = np.stack(tables).astype(np.float32)
    c, s = phases(np.arange(256), np.arange(256), 256, 1)
    out["w6"] = np.stack(split_np(np.concatenate([-s, c, s], axis=1) / 64.0))
    c, s = phases(np.arange(16), np.arange(256), 4096, 1)
    out["t6"] = np.stack([c, s]).astype(np.float32)
    return out


def split(value):
    high = value.astype(BF16)
    return high, (value - high.astype(F32)).astype(BF16)


def dot(a, b):
    return jnp.dot(a, b, preferred_element_type=F32)


def dot3(a, bh, bl):
    ah, al = split(a)
    return dot(ah, bh) + dot(ah, bl) + dot(al, bh)


def in_groups(rows, high, low, groups=GROUPS):
    size = len(rows) // groups
    out = []
    for group in range(groups):
        value = dot3(jnp.concatenate(rows[group * size : group * size + size], axis=0), high, low)
        height = rows[0].shape[0]
        out += [value[n * height : n * height + height] for n in range(size)]
    return out


def block_transpose(v):
    lane = lax.broadcasted_iota(jnp.int32, v[0].shape, 1)
    low64 = lane < 64
    low32 = (lane & 32) == 0
    a = [None] * 4
    for i in (0, 1):
        a[i] = jnp.where(low64, v[i], pltpu.roll(v[i + 2], 64, 1))
        a[i + 2] = jnp.where(low64, pltpu.roll(v[i], 64, 1), v[i + 2])
    o = [None] * 4
    for i in (0, 2):
        o[i] = jnp.where(low32, a[i], pltpu.roll(a[i + 1], 32, 1))
        o[i + 1] = jnp.where(low32, pltpu.roll(a[i], 96, 1), a[i + 1])
    return o


def range_kernel(raw_hbm, chirp_hbm, wa_hbm, wb_hbm, t1_hbm, out, raw, chirp, wa, wb, t1, turned_out, sem, raw_sem):
    copies = [
        pltpu.make_async_copy(source, target, sem.at[n])
        for n, (source, target) in enumerate(
            ((wa_hbm, wa), (t1_hbm, t1), (wb_hbm, wb), (chirp_hbm, chirp))
        )
    ]
    echoes = [
        [
            pltpu.make_async_copy(
                raw_hbm.at[p * 4 + channel], raw.at[p * 4 + channel], raw_sem.at[p * 4 + channel]
            )
            for p in range(4)
        ]
        for channel in range(4)
    ]
    copies[0].start()
    for copy in echoes[0]:
        copy.start()
    for copy in copies[1:]:
        copy.start()
    for channel in (1, 2, 3):
        for copy in echoes[channel]:
            copy.start()
    for channel in range(4):
        for copy in echoes[channel]:
            copy.wait()
    for copy in copies:
        copy.wait()
    spectra = []
    for channel in range(4):
        x = jnp.concatenate([raw[pulse * 4 + channel] for pulse in range(4)], axis=1)
        xh, xl = split(x)
        spectra.append(dot(wa[0], jnp.concatenate([xh, xl, xh], axis=0)))
    tr, ti = t1[0], t1[1]
    chirp_parts = []
    for part in (0, 1):
        natural = chirp[pl.ds(part, 64, stride=2), :]
        turned = natural.T
        chirp_parts.append(jnp.concatenate([turned[:64], turned[64:]], axis=1))
    cr, ci = chirp_parts
    rows = []
    for a in spectra:
        for pulse in range(4):
            ar = a[:64, pulse * 128 : pulse * 128 + 128]
            ai = a[64:, pulse * 128 : pulse * 128 + 128]
            rows.append(jnp.concatenate([ar * tr - ai * ti, ar * ti + ai * tr], axis=1))
    b = in_groups(rows, wb[0], wb[1])
    rows = []
    for row in range(16):
        br, bi = b[row][:, :128], b[row][:, 128:]
        rows.append(jnp.concatenate([br * cr + bi * ci, bi * cr - br * ci], axis=1))
    b = in_groups(rows, wb[2], wb[3])
    for channel in range(4):
        columns = []
        for row in range(channel * 4, channel * 4 + 4):
            br, bi = b[row][:, :128], b[row][:, 128:]
            columns.append(jnp.concatenate([br * tr + bi * ti, bi * tr - br * ti], axis=0))
        xh, xl = split(jnp.concatenate(columns, axis=1))
        a = dot(wa[1], jnp.concatenate([xh, xl, xh], axis=0))
        for part in (0, 1):
            o = block_transpose(
                [a[part * 64 : part * 64 + 64, p * 128 : p * 128 + 128] for p in range(4)]
            )
            for low in range(4):
                turned_out[pl.ds(low * 512 + channel * 2 + part, 64, stride=8), :] = o[low]
    results = [
        pltpu.make_async_copy(
            turned_out.at[pl.ds(low * 512, 512)].reshape(64, 8, 128), out.at[:, low], sem.at[low]
        )
        for low in range(4)
    ]
    for copy in results:
        copy.start()
    for copy in results:
        copy.wait()


def packed(value):
    whole = jnp.concatenate([jnp.broadcast_to(value[...], (8, 32))] * 4, axis=1)
    lane = lax.broadcasted_iota(jnp.int32, (8, 128), 1)
    row = lax.broadcasted_iota(jnp.int32, (8, 128), 0)
    return lanes_taken(whole, (lane & 15) + 16 * (row & 1))


def mixing_kernel(
    delays, reconstruction, rate, half, mig, mix, rate_out, half_out, mig_out, flat, turned
):
    rate_out[...] = packed(rate)
    half_out[...] = packed(half)
    mig_out[...] = packed(mig)
    channel = lax.broadcasted_iota(jnp.int32, (4, 1024), 0)
    frequency = lax.broadcasted_iota(jnp.int32, (4, 1024), 1)
    delay = jnp.where(
        channel < 2,
        jnp.where(channel < 1, delays[0], delays[1]),
        jnp.where(channel < 3, delays[2], delays[3]),
    )
    angle = (2.0 * math.pi / 1024) * ((frequency * delay) & 1023).astype(F32)
    cosine, sine = jnp.cos(angle), jnp.sin(angle)
    for band in range(4):
        real, imag = reconstruction[0, band], reconstruction[1, band]
        flat[band * 4 : band * 4 + 4, :] = real * cosine - imag * sine
        flat[16 + band * 4 : 16 + band * 4 + 4, :] = real * sine + imag * cosine
    for block in range(8):
        turned[block * 128 : block * 128 + 128, :] = flat[:, block * 128 : block * 128 + 128].T
    for high in range(4):
        for middle in range(4):
            pieces = [
                turned[pl.ds(high * 256 + middle * 4 + low, 16, stride=16), :] for low in range(4)
            ]
            at = high * 64 + middle * 16
            mix[at : at + 16, :] = jnp.concatenate(pieces, axis=1)


def azimuth_kernel(received, compact, w5, t5, unfolded, margin, g, mix):
    group = lax.broadcasted_iota(jnp.int32, (256, 128), 1) & 96

    def expand(entry, carry):
        mix[entry] = lanes_taken(compact[...], group + entry)
        return carry

    lax.fori_loop(0, 32, expand, 0, unroll=EXPAND)
    for pair in range(2):
        halves = []
        for part in (0, 1):
            z = jnp.concatenate(
                [
                    received[pl.ds(channel * 2 + part, 256, stride=8), :]
                    for channel in (2 * pair, 2 * pair + 1)
                ],
                axis=1,
            )
            zh, zl = split(z)
            rows = slice(256, 768) if part == 0 else slice(0, 512)
            halves.append(dot(w5[0, rows], zh) + dot(w5[0, rows], zl) + dot(w5[1, rows], zh))
        g[:, pair * 256 : pair * 256 + 256] = halves[0] + halves[1]

    def combine(middle, tile_half):
        start = middle * 16 + tile_half * 8
        spectrum = []
        for channel in range(4):
            parts = []
            for part in (0, 1):
                parts.append(
                    block_transpose(
                        [
                            g[
                                pl.ds(pl.multiple_of(part * 256 + low * 64 + start, 8), 8),
                                channel * 128 : channel * 128 + 128,
                            ]
                            for low in range(4)
                        ]
                    )
                )
            xr, xi = [parts[0][0]], [parts[1][0]]
            for pulse in (1, 2, 3):
                tr = t5[pulse - 1, 0, pl.ds(pl.multiple_of(start, 8), 8), :]
                ti = t5[pulse - 1, 1, pl.ds(pl.multiple_of(start, 8), 8), :]
                r, i = parts[0][pulse], parts[1][pulse]
                xr.append(r * tr - i * ti)
                xi.append(r * ti + i * tr)
            ar, ai = xr[0] + xr[2], xi[0] + xi[2]
            br, bi = xr[0] - xr[2], xi[0] - xi[2]
            er, ei = xr[1] + xr[3], xi[1] + xi[3]
            dr, di = xr[1] - xr[3], xi[1] - xi[3]
            spectrum.append(
                [(ar + er, ai + ei), (br + di, bi - dr), (ar - er, ai - ei), (br - di, bi + dr)]
            )
        for high in range(4):
            rows = pl.ds(pl.multiple_of(high * 64 + start, 8), 8)
            for band in range(4):
                real = imag = None
                for channel in range(4):
                    dr, di = spectrum[channel][high]
                    mr = mix[band * 4 + channel, rows, :]
                    mi = mix[16 + band * 4 + channel, rows, :]
                    r = mr * dr - mi * di
                    i = mr * di + mi * dr
                    real = r if real is None else real + r
                    imag = i if imag is None else imag + i
                to = band * 64 + high * 16 + tile_half * 8
                unfolded[middle, 0, to : to + 8, :] = real
                unfolded[middle, 1, to : to + 8, :] = imag

    def combine_all(middle, carry):
        combine(middle, 0)
        combine(middle, 1)
        return carry

    lax.fori_loop(0, 4, combine_all, 0, unroll=COMBINE)
    low16 = (lax.broadcasted_iota(jnp.int32, (256, 128), 1) & 16) == 0
    for middle in range(2):
        for part in (0, 1):
            margin[middle, part] = jnp.where(
                low16, unfolded[middle, part], pltpu.roll(unfolded[middle + 2, part], 16, 1)
            )


def mul_i(value, quarter):
    r, i = value
    return [(r, i), (-i, r), (-r, -i), (i, -r)][quarter % 4]


def add(a, b):
    return (a[0] + b[0], a[1] + b[1])


def sub(a, b):
    return (a[0] - b[0], a[1] - b[1])


def inverse4(x):
    a, b = add(x[0], x[2]), sub(x[0], x[2])
    e, d = add(x[1], x[3]), mul_i(sub(x[1], x[3]), 1)
    return [add(a, e), add(b, d), sub(a, e), sub(b, d)]


def lanes_taken(value, index):
    return jnp.take_along_axis(value, index, axis=1)


def to_image(f, w6, t6, y, image):
    def turned(a, b):
        return lax.dot_general(a, b, (((0,), (0,)), ((), ())), preferred_element_type=F32)

    fh, fl = f
    for middle in range(2):
        total = None
        for part, columns in ((0, slice(256, 768)), (1, slice(0, 512))):
            rows = slice(part * 256, part * 256 + 256)
            value = (
                turned(fh[middle, rows], w6[0, :, columns])
                + turned(fh[middle, rows], w6[1, :, columns])
                + turned(fl[middle, rows], w6[0, :, columns])
            )
            total = value if total is None else total + value
        y[middle] = total
    for column in range(2):
        for tile in range(2):
            inner = []
            for low in range(4):
                values = []
                for middle in range(4):
                    d1 = middle * 4 + low
                    at = low * 32 + middle // 2 * 16 + tile * 8
                    r = y[middle % 2, at : at + 8, column * 128 : column * 128 + 128]
                    i = y[middle % 2, at : at + 8, 256 + column * 128 : 256 + column * 128 + 128]
                    if d1:
                        tr = t6[0, d1 : d1 + 1, column * 128 : column * 128 + 128]
                        ti = t6[1, d1 : d1 + 1, column * 128 : column * 128 + 128]
                        r, i = r * tr - i * ti, r * ti + i * tr
                    values.append((r, i))
                inner.append(inverse4(values))
            for qa in range(4):
                values = []
                for low in range(4):
                    v = inner[low][qa]
                    turn = low * qa
                    if turn % 4 == 0:
                        v = mul_i(v, turn // 4)
                    else:
                        c = math.cos(2 * math.pi * turn / 16)
                        s = math.sin(2 * math.pi * turn / 16)
                        v = (v[0] * c - v[1] * s, v[0] * s + v[1] * c)
                    values.append(v)
                for qb, v in enumerate(inverse4(values)):
                    lanes = (qa + 4 * qb) * 256 + column * 128
                    image[0, tile * 8 : tile * 8 + 8, lanes : lanes + 128] = v[0]
                    image[1, tile * 8 : tile * 8 + 8, lanes : lanes + 128] = v[1]


def write_image(image, out, rows, sem):
    copies = [
        pltpu.make_async_copy(image.at[part], out.at[part, rows], sem.at[part]) for part in (0, 1)
    ]
    for copy in copies:
        copy.start()
    for copy in copies:
        copy.wait()


def tables(rate, half, mig, upper, middle, at):
    shape = (16, 128)
    lane = lax.broadcasted_iota(jnp.int32, shape, 1)
    row = lax.broadcasted_iota(jnp.int32, shape, 0)
    half_bit = lax.shift_right_logical(lane, 4) & 1
    width = jnp.broadcast_to(half[upper : upper + 1, :], shape)
    square = width * width
    inverse = 1.0 / square.astype(F32)
    moved = jnp.broadcast_to(mig[upper : upper + 1, :], shape)
    speed = jnp.broadcast_to(rate[upper : upper + 1, :], shape) * 16.0
    d = (row + at) * 16 + (half_bit * 2 + middle) * 4 + lax.shift_right_logical(lane, 5)
    centred = jnp.where(d >= 2048, d - 4096, d)
    c2 = centred * centred
    number = moved * jnp.minimum(c2, square) + lax.shift_right_logical(square, 1)
    shift = (number.astype(F32) * inverse).astype(jnp.int32)
    rest = number - shift * square
    shift = shift + jnp.where(rest >= square, 1, 0) - jnp.where(rest < 0, 1, 0)
    source = (lane & 15) + 16 * upper + shift
    turns = speed * (c2.astype(F32) * (1.0 / 4194304.0))
    turns = turns - jnp.floor(turns + 0.5)
    angle = turns * (2.0 * math.pi)
    inside = jnp.abs(centred) < width
    return source, jnp.where(inside, jnp.cos(angle), 0.0), jnp.where(inside, jnp.sin(angle), 0.0)


def lower_kernel(unfolded, rate, half, mig, w6, t6, out, kept, phase, index, fh, fl, y, image, sem):
    lane = lax.broadcasted_iota(jnp.int32, (16, 128), 1)
    second = (lane & 16) != 0
    for upper in (0, 1):
        for middle in range(2):
            for block in range(16):
                at = block * 16
                source, pr, pi = tables(rate, half, mig, upper, middle, at)
                lanes = (lane & 96) + (source & 31)
                values = []
                for part in (0, 1):
                    value = jnp.where(
                        second,
                        lanes_taken(unfolded[middle + 2, part, at : at + 16, :], lanes),
                        lanes_taken(unfolded[middle, part, at : at + 16, :], lanes),
                    )
                    if upper:
                        value = jnp.where(source >= 32, 0.0, value)
                    values.append(value)
                both = (values[0] * pr - values[1] * pi, values[0] * pi + values[1] * pr)
                if upper:
                    phase[middle, 0, at : at + 16, :] = jnp.where(source >= 32, pr, 0.0)
                    phase[middle, 1, at : at + 16, :] = jnp.where(source >= 32, pi, 0.0)
                    index[middle, at : at + 16, :] = (lane & 112) + (source & 15)
                for part, value in enumerate(both):
                    rows = slice(part * 256 + at, part * 256 + at + 16)
                    if upper:
                        kept[middle, rows, :] = value
                    else:
                        fh[middle, rows, :], fl[middle, rows, :] = split(value)
    to_image((fh, fl), w6, t6, y, image)
    write_image(image, out, slice(0, 16), sem)


def upper_kernel(margin, kept, phase, index, w6, t6, _, out, fh, fl, y, image, sem):
    for middle in range(2):
        for block in range(16):
            at = block * 16
            lanes = index[middle, at : at + 16, :]
            r = lanes_taken(margin[middle, 0, at : at + 16, :], lanes)
            i = lanes_taken(margin[middle, 1, at : at + 16, :], lanes)
            pr = phase[middle, 0, at : at + 16, :]
            pi = phase[middle, 1, at : at + 16, :]
            for part, value in enumerate((r * pr - i * pi, r * pi + i * pr)):
                rows = slice(part * 256 + at, part * 256 + at + 16)
                fh[middle, rows, :], fl[middle, rows, :] = split(value + kept[middle, rows, :])
    to_image((fh, fl), w6, t6, y, image)
    write_image(image, out, slice(16, 32), sem)


VMEM = pl.BlockSpec(memory_space=pltpu.VMEM)
SMEM = pl.BlockSpec(memory_space=pltpu.SMEM)
HBM = pl.BlockSpec(memory_space=pltpu.HBM)
MIB = 1 << 20


def call(kernel, out_shape, scratch, flops, operands, in_specs=None, out_specs=VMEM, limit=8, **more):
    return pl.pallas_call(
        kernel,
        out_shape=out_shape,
        in_specs=in_specs or [VMEM] * len(operands),
        out_specs=out_specs,
        scratch_shapes=scratch,
        compiler_params=pltpu.CompilerParams(vmem_limit_bytes=limit * MIB),
        cost_estimate=pl.CostEstimate(flops=flops, bytes_accessed=2 * MIB, transcendentals=0),
        **more,
    )(*operands)


def shape(*dims, dtype=F32):
    return jax.ShapeDtypeStruct(dims, dtype)


def local(raw, chirp, reconstruction, delays, rate, half, mig):
    k = constants()
    raw = raw.reshape(16, 2, 64, 128).transpose(0, 2, 1, 3).reshape(16, 128, 128)
    chirp = chirp.reshape(2, 64, 128).transpose(1, 0, 2).reshape(128, 128)
    dma = pltpu.SemaphoreType.DMA
    compressed = call(
        range_kernel, shape(64, 4, 8, 128),
        [
            pltpu.VMEM((16, 128, 128), F32),
            pltpu.VMEM((128, 128), F32),
            pltpu.VMEM((2, 128, 384), BF16),
            pltpu.VMEM((4, 256, 256), BF16),
            pltpu.VMEM((2, 64, 128), F32),
            pltpu.VMEM((2048, 128), F32),
            dma((4,)),
            dma((16,)),
        ],
        1 << 30, (raw, chirp, k["wa"], k["wb"], k["t1"]), in_specs=[HBM] * 5, out_specs=HBM, limit=63,
    )
    received = lax.all_to_all(compressed.reshape(256, 8, 128), AXES, 0, 0, tiled=True)
    received = received.reshape(2048, 128)
    integers = shape(8, 128, dtype=jnp.int32)
    mix, rate, half, mig = call(
        mixing_kernel, (shape(256, 128), shape(8, 128), integers, integers),
        [pltpu.VMEM((32, 1024), F32), pltpu.VMEM((1024, 32), F32)],
        1 << 24,
        (delays, reconstruction, rate.reshape(1, 32), half.reshape(1, 32), mig.reshape(1, 32)),
        in_specs=[SMEM] + [VMEM] * 4, out_specs=(VMEM,) * 4,
    )
    unfolded, margin = call(
        azimuth_kernel, (shape(4, 2, 256, 128), shape(2, 2, 256, 128)),
        [pltpu.VMEM((512, 512), F32), pltpu.VMEM((32, 256, 128), F32)],
        1 << 30, (received, mix, k["w5"], k["t5"]),
        out_specs=(VMEM, VMEM), limit=12,
    )
    pairs = [(i, i - 1) for i in range(1, lax.axis_size(AXES))]
    margin = lax.ppermute(margin, AXES, pairs)
    scratch = [
        pltpu.VMEM((2, 512, 128), BF16),
        pltpu.VMEM((2, 512, 128), BF16),
        pltpu.VMEM((2, 128, 512), F32),
        pltpu.VMEM((2, 16, 4096), F32),
        dma((2,)),
    ]
    image, kept, phase, index = call(
        lower_kernel,
        (
            shape(2, 32, 4096),
            shape(2, 512, 128),
            shape(2, 2, 256, 128),
            shape(2, 256, 128, dtype=jnp.int32),
        ),
        scratch, 1 << 30,
        (unfolded, rate, half, mig, k["w6"], k["t6"]),
        out_specs=(HBM, VMEM, VMEM, VMEM),
    )
    return call(
        upper_kernel, shape(2, 32, 4096), scratch, 1 << 30,
        (margin, kept, phase, index, k["w6"], k["t6"], image),
        in_specs=[VMEM] * 6 + [HBM], out_specs=HBM, input_output_aliases={6: 0},
    )


def solution(mesh):
    in_specs = (P(AXES, None, None, None), P(), P(), P(), P(AXES), P(AXES), P(AXES))
    return jax.shard_map(
        local, mesh=mesh, in_specs=in_specs, out_specs=P(None, AXES, None), check_vma=False
    )
```

```python
import functools
import math

import jax
import jax.numpy as jnp
import ml_dtypes
import numpy as np
from jax import lax
from jax.experimental import pallas as pl
from jax.experimental.pallas import tpu as pltpu
from jax.sharding import PartitionSpec as P

AXES = ("az", "rg")
GROUPS = 2
EXPAND = 8
F32 = jnp.float32
BF16 = jnp.bfloat16


def split_np(matrix):
    matrix = np.asarray(matrix, np.float64)
    high = matrix.astype(np.float32).astype(ml_dtypes.bfloat16)
    low = (matrix - high.astype(np.float64)).astype(np.float32).astype(ml_dtypes.bfloat16)
    return high, low


def phases(rows, columns, length, sign):
    turns = np.outer(np.asarray(rows), np.asarray(columns)) % length
    angle = sign * 2.0 * np.pi * turns / length
    return np.cos(angle), np.sin(angle)


def complex_left(cosine, sine):
    return np.block([[cosine, -sine], [sine, cosine]])


@functools.lru_cache(None)
def constants():
    out = {}
    c, s = phases(np.arange(64), np.arange(64), 64, -1)
    m = complex_left(c, s).reshape(128, 2, 64).transpose(0, 2, 1).reshape(128, 128)
    h, l = split_np(m)
    first = np.concatenate([h, h, l], axis=1)
    c, s = phases(np.arange(64), np.arange(64), 64, 1)
    h, l = split_np(complex_left(c, s) / 8192.0)
    out["wa"] = np.stack([first, np.concatenate([h, h, l], axis=1)])
    order = np.arange(128).reshape(64, 2).T.reshape(-1)
    c, s = phases(np.arange(128), order, 128, -1)
    pair = split_np(np.block([[c, s], [-s, c]]))
    c, s = phases(order, np.arange(128), 128, 1)
    out["wb"] = np.stack(pair + split_np(np.block([[c, s], [-s, c]])))
    c, s = phases(np.arange(64), np.arange(128), 8192, -1)
    out["t1"] = np.stack([c, s]).astype(np.float32)
    fm = np.arange(256).reshape(16, 4, 4).transpose(2, 1, 0).reshape(-1)
    c, s = phases(fm, np.arange(256), 256, 1)
    out["w5"] = np.stack(split_np(np.concatenate([s, c, -s], axis=0) / 32.0))
    grid = fm.reshape(4, 64)
    tables = []
    for pulse in (1, 2, 3):
        angle = -2.0 * np.pi * (pulse * grid % 1024) / 1024
        angle = np.repeat(angle.T, 32, axis=1)
        tables.append(np.stack([np.cos(angle), np.sin(angle)]))
    out["t5"] = np.stack(tables).astype(np.float32)
    c, s = phases(np.arange(256), np.arange(256), 256, 1)
    out["w6"] = np.stack(split_np(np.concatenate([-s, c, s], axis=1) / 64.0))
    c, s = phases(np.arange(16), np.arange(256), 4096, 1)
    out["t6"] = np.stack([c, s]).astype(np.float32)
    return out


def split(value):
    high = value.astype(BF16)
    return high, (value - high.astype(F32)).astype(BF16)


def dot(a, b):
    return jnp.dot(a, b, preferred_element_type=F32)


def dot3(a, bh, bl):
    ah, al = split(a)
    return dot(ah, bh) + dot(ah, bl) + dot(al, bh)


def in_groups(rows, high, low, groups=GROUPS):
    size = len(rows) // groups
    out = []
    for group in range(groups):
        value = dot3(jnp.concatenate(rows[group * size : group * size + size], axis=0), high, low)
        height = rows[0].shape[0]
        out += [value[n * height : n * height + height] for n in range(size)]
    return out


def block_transpose(v):
    lane = lax.broadcasted_iota(jnp.int32, v[0].shape, 1)
    low64 = lane < 64
    low32 = (lane & 32) == 0
    a = [None] * 4
    for i in (0, 1):
        a[i] = jnp.where(low64, v[i], pltpu.roll(v[i + 2], 64, 1))
        a[i + 2] = jnp.where(low64, pltpu.roll(v[i], 64, 1), v[i + 2])
    o = [None] * 4
    for i in (0, 2):
        o[i] = jnp.where(low32, a[i], pltpu.roll(a[i + 1], 32, 1))
        o[i + 1] = jnp.where(low32, pltpu.roll(a[i], 96, 1), a[i + 1])
    return o


def range_kernel(raw_hbm, chirp_hbm, wa_hbm, wb_hbm, t1_hbm, out, raw, chirp, wa, wb, t1, turned_out, sem, raw_sem):
    copies = [
        pltpu.make_async_copy(source, target, sem.at[n])
        for n, (source, target) in enumerate(
            ((wa_hbm, wa), (t1_hbm, t1), (wb_hbm, wb), (chirp_hbm, chirp))
        )
    ]
    echoes = [
        [
            pltpu.make_async_copy(
                raw_hbm.at[p * 4 + channel], raw.at[p * 4 + channel], raw_sem.at[p * 4 + channel]
            )
            for p in range(4)
        ]
        for channel in range(4)
    ]
    copies[0].start()
    for copy in echoes[0]:
        copy.start()
    for copy in copies[1:]:
        copy.start()
    for channel in (1, 2, 3):
        for copy in echoes[channel]:
            copy.start()
    for channel in range(4):
        for copy in echoes[channel]:
            copy.wait()
    for copy in copies:
        copy.wait()
    spectra = []
    for channel in range(4):
        x = jnp.concatenate([raw[pulse * 4 + channel] for pulse in range(4)], axis=1)
        xh, xl = split(x)
        spectra.append(dot(wa[0], jnp.concatenate([xh, xl, xh], axis=0)))
    tr, ti = t1[0], t1[1]
    chirp_parts = []
    for part in (0, 1):
        natural = chirp[pl.ds(part, 64, stride=2), :]
        turned = natural.T
        chirp_parts.append(jnp.concatenate([turned[:64], turned[64:]], axis=1))
    cr, ci = chirp_parts
    rows = []
    for a in spectra:
        for pulse in range(4):
            ar = a[:64, pulse * 128 : pulse * 128 + 128]
            ai = a[64:, pulse * 128 : pulse * 128 + 128]
            rows.append(jnp.concatenate([ar * tr - ai * ti, ar * ti + ai * tr], axis=1))
    b = in_groups(rows, wb[0], wb[1])
    rows = []
    for row in range(16):
        br, bi = b[row][:, :128], b[row][:, 128:]
        rows.append(jnp.concatenate([br * cr + bi * ci, bi * cr - br * ci], axis=1))
    b = in_groups(rows, wb[2], wb[3])
    for channel in range(4):
        columns = []
        for row in range(channel * 4, channel * 4 + 4):
            br, bi = b[row][:, :128], b[row][:, 128:]
            columns.append(jnp.concatenate([br * tr + bi * ti, bi * tr - br * ti], axis=0))
        xh, xl = split(jnp.concatenate(columns, axis=1))
        a = dot(wa[1], jnp.concatenate([xh, xl, xh], axis=0))
        for part in (0, 1):
            o = block_transpose(
                [a[part * 64 : part * 64 + 64, p * 128 : p * 128 + 128] for p in range(4)]
            )
            for low in range(4):
                turned_out[pl.ds(low * 512 + channel * 2 + part, 64, stride=8), :] = o[low]
    results = [
        pltpu.make_async_copy(
            turned_out.at[pl.ds(low * 512, 512)].reshape(64, 8, 128), out.at[:, low], sem.at[low]
        )
        for low in range(4)
    ]
    for copy in results:
        copy.start()
    for copy in results:
        copy.wait()


def packed(value):
    whole = jnp.concatenate([jnp.broadcast_to(value[...], (8, 32))] * 4, axis=1)
    lane = lax.broadcasted_iota(jnp.int32, (8, 128), 1)
    row = lax.broadcasted_iota(jnp.int32, (8, 128), 0)
    return lanes_taken(whole, (lane & 15) + 16 * (row & 1))


def mixing_kernel(
    delays, reconstruction, rate, half, mig, mix, rate_out, half_out, mig_out, flat, turned
):
    rate_out[...] = packed(rate)
    half_out[...] = packed(half)
    mig_out[...] = packed(mig)
    channel = lax.broadcasted_iota(jnp.int32, (4, 1024), 0)
    frequency = lax.broadcasted_iota(jnp.int32, (4, 1024), 1)
    delay = jnp.where(
        channel < 2,
        jnp.where(channel < 1, delays[0], delays[1]),
        jnp.where(channel < 3, delays[2], delays[3]),
    )
    angle = (2.0 * math.pi / 1024) * ((frequency * delay) & 1023).astype(F32)
    cosine, sine = jnp.cos(angle), jnp.sin(angle)
    for band in range(4):
        real, imag = reconstruction[0, band], reconstruction[1, band]
        flat[band * 4 : band * 4 + 4, :] = real * cosine - imag * sine
        flat[16 + band * 4 : 16 + band * 4 + 4, :] = real * sine + imag * cosine
    for block in range(8):
        turned[block * 128 : block * 128 + 128, :] = flat[:, block * 128 : block * 128 + 128].T
    for high in range(4):
        for middle in range(4):
            pieces = [
                turned[pl.ds(high * 256 + middle * 4 + low, 16, stride=16), :] for low in range(4)
            ]
            at = high * 64 + middle * 16
            mix[at : at + 16, :] = jnp.concatenate(pieces, axis=1)


def azimuth_kernel(received, w5, t5, spectrum, margin, g):
    for pair in range(2):
        halves = []
        for part in (0, 1):
            z = jnp.concatenate(
                [
                    received[pl.ds(channel * 2 + part, 256, stride=8), :]
                    for channel in (2 * pair, 2 * pair + 1)
                ],
                axis=1,
            )
            zh, zl = split(z)
            rows = slice(256, 768) if part == 0 else slice(0, 512)
            halves.append(dot(w5[0, rows], zh) + dot(w5[0, rows], zl) + dot(w5[1, rows], zh))
        g[:, pair * 256 : pair * 256 + 256] = halves[0] + halves[1]
    low16 = (lax.broadcasted_iota(jnp.int32, (8, 128), 1) & 16) == 0

    def bins(channel, start):
        parts = []
        for part in (0, 1):
            parts.append(
                block_transpose(
                    [
                        g[
                            part * 256 + low * 64 + start : part * 256 + low * 64 + start + 8,
                            channel * 128 : channel * 128 + 128,
                        ]
                        for low in range(4)
                    ]
                )
            )
        xr, xi = [parts[0][0]], [parts[1][0]]
        for pulse in (1, 2, 3):
            tr = t5[pulse - 1, 0, start : start + 8, :]
            ti = t5[pulse - 1, 1, start : start + 8, :]
            r, i = parts[0][pulse], parts[1][pulse]
            xr.append(r * tr - i * ti)
            xi.append(r * ti + i * tr)
        ar, ai = xr[0] + xr[2], xi[0] + xi[2]
        br, bi = xr[0] - xr[2], xi[0] - xi[2]
        er, ei = xr[1] + xr[3], xi[1] + xi[3]
        dr, di = xr[1] - xr[3], xi[1] - xi[3]
        return [(ar + er, ai + ei), (br + di, bi - dr), (ar - er, ai - ei), (br - di, bi + dr)]

    for channel in range(4):
        for middle in range(2):
            for tile_half in range(2):
                starts = [(middle + 2 * n) * 16 + tile_half * 8 for n in (0, 1)]
                values = [bins(channel, start) for start in starts]
                for high in range(4):
                    for part in (0, 1):
                        for n in (0, 1):
                            at = high * 64 + starts[n]
                            spectrum[channel, part, at : at + 8, :] = values[n][high][part]
                        at = high * 16 + tile_half * 8
                        margin[channel, part, middle, at : at + 8, :] = jnp.where(
                            low16, values[0][high][part], pltpu.roll(values[1][high][part], 16, 1)
                        )


def mixed(entries, values):
    real = imag = None
    for (mr, mi), (dr, di) in zip(entries, values):
        r = mr * dr - mi * di
        i = mr * di + mi * dr
        real = r if real is None else real + r
        imag = i if imag is None else imag + i
    return real, imag


def unfold_kernel(spectrum, compact, unfolded, packed_mix, mix):
    group = lax.broadcasted_iota(jnp.int32, (256, 128), 1) & 96

    def expand(entry, carry):
        mix[entry] = lanes_taken(compact[...], group + entry)
        return carry

    lax.fori_loop(0, 32, expand, 0, unroll=EXPAND)
    low16 = (lax.broadcasted_iota(jnp.int32, (16, 128), 1) & 16) == 0

    def pack(entry, carry):
        for middle in range(2):
            for high in range(4):
                at = high * 64 + middle * 16
                packed_mix[entry, middle, high * 16 : high * 16 + 16, :] = jnp.where(
                    low16, mix[entry, at : at + 16, :], mix[entry, at + 32 : at + 48, :]
                )
        return carry

    lax.fori_loop(0, 32, pack, 0, unroll=2)

    def combine(middle, carry):
        for high in range(4):
            for tile_half in range(2):
                rows = pl.ds(pl.multiple_of(high * 64 + middle * 16 + tile_half * 8, 8), 8)
                values = [(spectrum[c, 0, rows, :], spectrum[c, 1, rows, :]) for c in range(4)]
                for band in range(4):
                    entries = [
                        (mix[band * 4 + c, rows, :], mix[16 + band * 4 + c, rows, :])
                        for c in range(4)
                    ]
                    to = band * 64 + high * 16 + tile_half * 8
                    real, imag = mixed(entries, values)
                    unfolded[middle, 0, to : to + 8, :] = real
                    unfolded[middle, 1, to : to + 8, :] = imag
        return carry

    lax.fori_loop(0, 4, combine, 0)


def mul_i(value, quarter):
    r, i = value
    return [(r, i), (-i, r), (-r, -i), (i, -r)][quarter % 4]


def add(a, b):
    return (a[0] + b[0], a[1] + b[1])


def sub(a, b):
    return (a[0] - b[0], a[1] - b[1])


def inverse4(x):
    a, b = add(x[0], x[2]), sub(x[0], x[2])
    e, d = add(x[1], x[3]), mul_i(sub(x[1], x[3]), 1)
    return [add(a, e), add(b, d), sub(a, e), sub(b, d)]


def lanes_taken(value, index):
    return jnp.take_along_axis(value, index, axis=1)


def to_image(f, w6, t6, y, image):
    def turned(a, b):
        return lax.dot_general(a, b, (((0,), (0,)), ((), ())), preferred_element_type=F32)

    fh, fl = f
    for middle in range(2):
        total = None
        for part, columns in ((0, slice(256, 768)), (1, slice(0, 512))):
            rows = slice(part * 256, part * 256 + 256)
            value = (
                turned(fh[middle, rows], w6[0, :, columns])
                + turned(fh[middle, rows], w6[1, :, columns])
                + turned(fl[middle, rows], w6[0, :, columns])
            )
            total = value if total is None else total + value
        y[middle] = total
    for column in range(2):
        for tile in range(2):
            inner = []
            for low in range(4):
                values = []
                for middle in range(4):
                    d1 = middle * 4 + low
                    at = low * 32 + middle // 2 * 16 + tile * 8
                    r = y[middle % 2, at : at + 8, column * 128 : column * 128 + 128]
                    i = y[middle % 2, at : at + 8, 256 + column * 128 : 256 + column * 128 + 128]
                    if d1:
                        tr = t6[0, d1 : d1 + 1, column * 128 : column * 128 + 128]
                        ti = t6[1, d1 : d1 + 1, column * 128 : column * 128 + 128]
                        r, i = r * tr - i * ti, r * ti + i * tr
                    values.append((r, i))
                inner.append(inverse4(values))
            for qa in range(4):
                values = []
                for low in range(4):
                    v = inner[low][qa]
                    turn = low * qa
                    if turn % 4 == 0:
                        v = mul_i(v, turn // 4)
                    else:
                        c = math.cos(2 * math.pi * turn / 16)
                        s = math.sin(2 * math.pi * turn / 16)
                        v = (v[0] * c - v[1] * s, v[0] * s + v[1] * c)
                    values.append(v)
                for qb, v in enumerate(inverse4(values)):
                    lanes = (qa + 4 * qb) * 256 + column * 128
                    image[0, tile * 8 : tile * 8 + 8, lanes : lanes + 128] = v[0]
                    image[1, tile * 8 : tile * 8 + 8, lanes : lanes + 128] = v[1]


def write_image(image, out, rows, sem):
    copies = [
        pltpu.make_async_copy(image.at[part], out.at[part, rows], sem.at[part]) for part in (0, 1)
    ]
    for copy in copies:
        copy.start()
    for copy in copies:
        copy.wait()


def tables(rate, half, mig, upper, middle, at):
    shape = (16, 128)
    lane = lax.broadcasted_iota(jnp.int32, shape, 1)
    row = lax.broadcasted_iota(jnp.int32, shape, 0)
    half_bit = lax.shift_right_logical(lane, 4) & 1
    width = jnp.broadcast_to(half[upper : upper + 1, :], shape)
    square = width * width
    inverse = 1.0 / square.astype(F32)
    moved = jnp.broadcast_to(mig[upper : upper + 1, :], shape)
    speed = jnp.broadcast_to(rate[upper : upper + 1, :], shape) * 16.0
    d = (row + at) * 16 + (half_bit * 2 + middle) * 4 + lax.shift_right_logical(lane, 5)
    centred = jnp.where(d >= 2048, d - 4096, d)
    c2 = centred * centred
    number = moved * jnp.minimum(c2, square) + lax.shift_right_logical(square, 1)
    shift = (number.astype(F32) * inverse).astype(jnp.int32)
    rest = number - shift * square
    shift = shift + jnp.where(rest >= square, 1, 0) - jnp.where(rest < 0, 1, 0)
    source = (lane & 15) + 16 * upper + shift
    turns = speed * (c2.astype(F32) * (1.0 / 4194304.0))
    turns = turns - jnp.floor(turns + 0.5)
    angle = turns * (2.0 * math.pi)
    inside = jnp.abs(centred) < width
    return source, jnp.where(inside, jnp.cos(angle), 0.0), jnp.where(inside, jnp.sin(angle), 0.0)


def lower_kernel(unfolded, rate, half, mig, w6, t6, out, kept, phase, index, fh, fl, y, image, sem):
    lane = lax.broadcasted_iota(jnp.int32, (16, 128), 1)
    second = (lane & 16) != 0
    for upper in (0, 1):
        for middle in range(2):
            for block in range(16):
                at = block * 16
                source, pr, pi = tables(rate, half, mig, upper, middle, at)
                lanes = (lane & 96) + (source & 31)
                values = []
                for part in (0, 1):
                    value = jnp.where(
                        second,
                        lanes_taken(unfolded[middle + 2, part, at : at + 16, :], lanes),
                        lanes_taken(unfolded[middle, part, at : at + 16, :], lanes),
                    )
                    if upper:
                        value = jnp.where(source >= 32, 0.0, value)
                    values.append(value)
                both = (values[0] * pr - values[1] * pi, values[0] * pi + values[1] * pr)
                if upper:
                    phase[middle, 0, at : at + 16, :] = jnp.where(source >= 32, pr, 0.0)
                    phase[middle, 1, at : at + 16, :] = jnp.where(source >= 32, pi, 0.0)
                    index[middle, at : at + 16, :] = (lane & 112) + (source & 15)
                for part, value in enumerate(both):
                    rows = slice(part * 256 + at, part * 256 + at + 16)
                    if upper:
                        kept[middle, rows, :] = value
                    else:
                        fh[middle, rows, :], fl[middle, rows, :] = split(value)
    to_image((fh, fl), w6, t6, y, image)
    write_image(image, out, slice(0, 16), sem)


def upper_kernel(
    margin, packed_mix, kept, phase, index, w6, t6, _, out, fh, fl, y, image, sem
):
    for middle in range(2):
        for high in range(4):
            rows = slice(high * 16, high * 16 + 16)
            values = [(margin[c, 0, middle, rows, :], margin[c, 1, middle, rows, :]) for c in range(4)]
            for band in range(4):
                entries = [
                    (
                        packed_mix[band * 4 + c, middle, rows, :],
                        packed_mix[16 + band * 4 + c, middle, rows, :],
                    )
                    for c in range(4)
                ]
                at = band * 64 + high * 16
                lanes = index[middle, at : at + 16, :]
                r, i = [lanes_taken(value, lanes) for value in mixed(entries, values)]
                pr = phase[middle, 0, at : at + 16, :]
                pi = phase[middle, 1, at : at + 16, :]
                for part, value in enumerate((r * pr - i * pi, r * pi + i * pr)):
                    to = slice(part * 256 + at, part * 256 + at + 16)
                    fh[middle, to, :], fl[middle, to, :] = split(value + kept[middle, to, :])
    to_image((fh, fl), w6, t6, y, image)
    write_image(image, out, slice(16, 32), sem)


VMEM = pl.BlockSpec(memory_space=pltpu.VMEM)
SMEM = pl.BlockSpec(memory_space=pltpu.SMEM)
HBM = pl.BlockSpec(memory_space=pltpu.HBM)
MIB = 1 << 20


def call(kernel, out_shape, scratch, flops, operands, in_specs=None, out_specs=VMEM, limit=8, **more):
    return pl.pallas_call(
        kernel,
        out_shape=out_shape,
        in_specs=in_specs or [VMEM] * len(operands),
        out_specs=out_specs,
        scratch_shapes=scratch,
        compiler_params=pltpu.CompilerParams(vmem_limit_bytes=limit * MIB),
        cost_estimate=pl.CostEstimate(flops=flops, bytes_accessed=2 * MIB, transcendentals=0),
        **more,
    )(*operands)


def shape(*dims, dtype=F32):
    return jax.ShapeDtypeStruct(dims, dtype)


def local(raw, chirp, reconstruction, delays, rate, half, mig):
    k = constants()
    raw = raw.reshape(16, 2, 64, 128).transpose(0, 2, 1, 3).reshape(16, 128, 128)
    chirp = chirp.reshape(2, 64, 128).transpose(1, 0, 2).reshape(128, 128)
    dma = pltpu.SemaphoreType.DMA
    compressed = call(
        range_kernel, shape(64, 4, 8, 128),
        [
            pltpu.VMEM((16, 128, 128), F32),
            pltpu.VMEM((128, 128), F32),
            pltpu.VMEM((2, 128, 384), BF16),
            pltpu.VMEM((4, 256, 256), BF16),
            pltpu.VMEM((2, 64, 128), F32),
            pltpu.VMEM((2048, 128), F32),
            dma((4,)),
            dma((16,)),
        ],
        1 << 30, (raw, chirp, k["wa"], k["wb"], k["t1"]), in_specs=[HBM] * 5, out_specs=HBM, limit=63,
    )
    received = lax.all_to_all(compressed.reshape(256, 8, 128), AXES, 0, 0, tiled=True)
    received = received.reshape(2048, 128)
    integers = shape(8, 128, dtype=jnp.int32)
    mix, rate, half, mig = call(
        mixing_kernel, (shape(256, 128), shape(8, 128), integers, integers),
        [pltpu.VMEM((32, 1024), F32), pltpu.VMEM((1024, 32), F32)],
        1 << 24,
        (delays, reconstruction, rate.reshape(1, 32), half.reshape(1, 32), mig.reshape(1, 32)),
        in_specs=[SMEM] + [VMEM] * 4, out_specs=(VMEM,) * 4,
    )
    spectrum, margin = call(
        azimuth_kernel, (shape(4, 2, 256, 128), shape(4, 2, 2, 64, 128)),
        [pltpu.VMEM((512, 512), F32)],
        1 << 30, (received, k["w5"], k["t5"]), out_specs=(VMEM, VMEM),
    )
    pairs = [(i, i - 1) for i in range(1, lax.axis_size(AXES))]
    margin = lax.ppermute(margin, AXES, pairs)
    unfolded, packed_mix = call(
        unfold_kernel, (shape(4, 2, 256, 128), shape(32, 2, 64, 128)),
        [pltpu.VMEM((32, 256, 128), F32)],
        1 << 30, (spectrum, mix), out_specs=(VMEM, VMEM), limit=12,
    )
    scratch = [
        pltpu.VMEM((2, 512, 128), BF16),
        pltpu.VMEM((2, 512, 128), BF16),
        pltpu.VMEM((2, 128, 512), F32),
        pltpu.VMEM((2, 16, 4096), F32),
        dma((2,)),
    ]
    image, kept, phase, index = call(
        lower_kernel,
        (
            shape(2, 32, 4096),
            shape(2, 512, 128),
            shape(2, 2, 256, 128),
            shape(2, 256, 128, dtype=jnp.int32),
        ),
        scratch, 1 << 30,
        (unfolded, rate, half, mig, k["w6"], k["t6"]),
        out_specs=(HBM, VMEM, VMEM, VMEM),
    )
    return call(
        upper_kernel, shape(2, 32, 4096), scratch, 1 << 30,
        (margin, packed_mix, kept, phase, index, k["w6"], k["t6"], image),
        in_specs=[VMEM] * 7 + [HBM], out_specs=HBM, input_output_aliases={7: 0},
    )


def solution(mesh):
    in_specs = (P(AXES, None, None, None), P(), P(), P(), P(AXES), P(AXES), P(AXES))
    return jax.shard_map(
        local, mesh=mesh, in_specs=in_specs, out_specs=P(None, AXES, None), check_vma=False
    )
```

```python
import functools
import math

import jax
import jax.numpy as jnp
import ml_dtypes
import numpy as np
from jax import lax
from jax.experimental import pallas as pl
from jax.experimental.pallas import tpu as pltpu
from jax.sharding import PartitionSpec as P

AXES = ("az", "rg")
GROUPS = 2
EXPAND = 8
F32 = jnp.float32
BF16 = jnp.bfloat16


def split_np(matrix):
    matrix = np.asarray(matrix, np.float64)
    high = matrix.astype(np.float32).astype(ml_dtypes.bfloat16)
    low = (matrix - high.astype(np.float64)).astype(np.float32).astype(ml_dtypes.bfloat16)
    return high, low


def phases(rows, columns, length, sign):
    turns = np.outer(np.asarray(rows), np.asarray(columns)) % length
    angle = sign * 2.0 * np.pi * turns / length
    return np.cos(angle), np.sin(angle)


def complex_left(cosine, sine):
    return np.block([[cosine, -sine], [sine, cosine]])


@functools.lru_cache(None)
def constants():
    out = {}
    c, s = phases(np.arange(64), np.arange(64), 64, -1)
    m = complex_left(c, s).reshape(128, 2, 64).transpose(0, 2, 1).reshape(128, 128)
    h, l = split_np(m)
    first = np.concatenate([h, h, l], axis=1)
    c, s = phases(np.arange(64), np.arange(64), 64, 1)
    h, l = split_np(complex_left(c, s) / 8192.0)
    out["wa"] = np.stack([first, np.concatenate([h, h, l], axis=1)])
    order = np.arange(128).reshape(64, 2).T.reshape(-1)
    c, s = phases(np.arange(128), order, 128, -1)
    pair = split_np(np.block([[c, s], [-s, c]]))
    c, s = phases(order, np.arange(128), 128, 1)
    out["wb"] = np.stack(pair + split_np(np.block([[c, s], [-s, c]])))
    c, s = phases(np.arange(64), np.arange(128), 8192, -1)
    out["t1"] = np.stack([c, s]).astype(np.float32)
    fm = np.arange(256).reshape(16, 4, 4).transpose(2, 1, 0)
    sets = []
    for middle in range(2):
        c, s = phases(fm[:, middle::2].reshape(-1), np.arange(256), 256, 1)
        sets.append(np.concatenate([s, c, -s], axis=0) / 32.0)
    for middle in range(2):
        out[f"w5{middle}"] = np.stack(split_np(sets[middle]))
    fm = fm.reshape(-1)
    grid = fm.reshape(4, 64)
    tables = []
    for pulse in (1, 2, 3):
        angle = -2.0 * np.pi * (pulse * grid % 1024) / 1024
        angle = np.repeat(angle.T, 32, axis=1)
        tables.append(np.stack([np.cos(angle), np.sin(angle)]))
    out["t5"] = np.stack(tables).astype(np.float32)
    c, s = phases(np.arange(256), np.arange(256), 256, 1)
    out["w6"] = np.stack(split_np(np.concatenate([-s, c, s], axis=1) / 64.0))
    c, s = phases(np.arange(16), np.arange(256), 4096, 1)
    out["t6"] = np.stack([c, s]).astype(np.float32)
    return out


def split(value):
    high = value.astype(BF16)
    return high, (value - high.astype(F32)).astype(BF16)


def dot(a, b):
    return jnp.dot(a, b, preferred_element_type=F32)


def dot3(a, bh, bl):
    ah, al = split(a)
    return dot(ah, bh) + dot(ah, bl) + dot(al, bh)


def in_groups(rows, high, low, groups=GROUPS):
    size = len(rows) // groups
    out = []
    for group in range(groups):
        value = dot3(jnp.concatenate(rows[group * size : group * size + size], axis=0), high, low)
        height = rows[0].shape[0]
        out += [value[n * height : n * height + height] for n in range(size)]
    return out


def block_transpose(v):
    lane = lax.broadcasted_iota(jnp.int32, v[0].shape, 1)
    low64 = lane < 64
    low32 = (lane & 32) == 0
    a = [None] * 4
    for i in (0, 1):
        a[i] = jnp.where(low64, v[i], pltpu.roll(v[i + 2], 64, 1))
        a[i + 2] = jnp.where(low64, pltpu.roll(v[i], 64, 1), v[i + 2])
    o = [None] * 4
    for i in (0, 2):
        o[i] = jnp.where(low32, a[i], pltpu.roll(a[i + 1], 32, 1))
        o[i + 1] = jnp.where(low32, pltpu.roll(a[i], 96, 1), a[i + 1])
    return o


def range_kernel(raw_hbm, chirp_hbm, wa_hbm, wb_hbm, t1_hbm, out, raw, chirp, wa, wb, t1, turned_out, sem, raw_sem):
    copies = [
        pltpu.make_async_copy(source, target, sem.at[n])
        for n, (source, target) in enumerate(
            ((wa_hbm, wa), (t1_hbm, t1), (wb_hbm, wb), (chirp_hbm, chirp))
        )
    ]
    echoes = [
        [
            pltpu.make_async_copy(
                raw_hbm.at[p * 4 + channel], raw.at[p * 4 + channel], raw_sem.at[p * 4 + channel]
            )
            for p in range(4)
        ]
        for channel in range(4)
    ]
    copies[0].start()
    for copy in echoes[0]:
        copy.start()
    for copy in copies[1:]:
        copy.start()
    for channel in (1, 2, 3):
        for copy in echoes[channel]:
            copy.start()
    for channel in range(4):
        for copy in echoes[channel]:
            copy.wait()
    for copy in copies:
        copy.wait()
    spectra = []
    for channel in range(4):
        x = jnp.concatenate([raw[pulse * 4 + channel] for pulse in range(4)], axis=1)
        xh, xl = split(x)
        spectra.append(dot(wa[0], jnp.concatenate([xh, xl, xh], axis=0)))
    tr, ti = t1[0], t1[1]
    chirp_parts = []
    for part in (0, 1):
        natural = chirp[pl.ds(part, 64, stride=2), :]
        turned = natural.T
        chirp_parts.append(jnp.concatenate([turned[:64], turned[64:]], axis=1))
    cr, ci = chirp_parts
    rows = []
    for a in spectra:
        for pulse in range(4):
            ar = a[:64, pulse * 128 : pulse * 128 + 128]
            ai = a[64:, pulse * 128 : pulse * 128 + 128]
            rows.append(jnp.concatenate([ar * tr - ai * ti, ar * ti + ai * tr], axis=1))
    b = in_groups(rows, wb[0], wb[1])
    rows = []
    for row in range(16):
        br, bi = b[row][:, :128], b[row][:, 128:]
        rows.append(jnp.concatenate([br * cr + bi * ci, bi * cr - br * ci], axis=1))
    b = in_groups(rows, wb[2], wb[3])
    for channel in range(4):
        columns = []
        for row in range(channel * 4, channel * 4 + 4):
            br, bi = b[row][:, :128], b[row][:, 128:]
            columns.append(jnp.concatenate([br * tr + bi * ti, bi * tr - br * ti], axis=0))
        xh, xl = split(jnp.concatenate(columns, axis=1))
        a = dot(wa[1], jnp.concatenate([xh, xl, xh], axis=0))
        for part in (0, 1):
            o = block_transpose(
                [a[part * 64 : part * 64 + 64, p * 128 : p * 128 + 128] for p in range(4)]
            )
            for low in range(4):
                turned_out[pl.ds(low * 512 + channel * 2 + part, 64, stride=8), :] = o[low]
    results = [
        pltpu.make_async_copy(
            turned_out.at[pl.ds(low * 512, 512)].reshape(64, 8, 128), out.at[:, low], sem.at[low]
        )
        for low in range(4)
    ]
    for copy in results:
        copy.start()
    for copy in results:
        copy.wait()


def packed(value):
    whole = jnp.concatenate([jnp.broadcast_to(value[...], (8, 32))] * 4, axis=1)
    lane = lax.broadcasted_iota(jnp.int32, (8, 128), 1)
    row = lax.broadcasted_iota(jnp.int32, (8, 128), 0)
    return lanes_taken(whole, (lane & 15) + 16 * (row & 1))


def mixing_kernel(
    delays, reconstruction, rate, half, mig, mix, rate_out, half_out, mig_out, flat, turned
):
    rate_out[...] = packed(rate)
    half_out[...] = packed(half)
    mig_out[...] = packed(mig)
    channel = lax.broadcasted_iota(jnp.int32, (4, 1024), 0)
    frequency = lax.broadcasted_iota(jnp.int32, (4, 1024), 1)
    delay = jnp.where(
        channel < 2,
        jnp.where(channel < 1, delays[0], delays[1]),
        jnp.where(channel < 3, delays[2], delays[3]),
    )
    angle = (2.0 * math.pi / 1024) * ((frequency * delay) & 1023).astype(F32)
    cosine, sine = jnp.cos(angle), jnp.sin(angle)
    for band in range(4):
        real, imag = reconstruction[0, band], reconstruction[1, band]
        flat[band * 4 : band * 4 + 4, :] = real * cosine - imag * sine
        flat[16 + band * 4 : 16 + band * 4 + 4, :] = real * sine + imag * cosine
    for block in range(8):
        turned[block * 128 : block * 128 + 128, :] = flat[:, block * 128 : block * 128 + 128].T
    for high in range(4):
        for middle in range(4):
            pieces = [
                turned[pl.ds(high * 256 + middle * 4 + low, 16, stride=16), :] for low in range(4)
            ]
            at = high * 64 + middle * 16
            mix[at : at + 16, :] = jnp.concatenate(pieces, axis=1)


def azimuth_kernel(middle, received, w5, t5, spectrum, margin, g):
    for pair in range(2):
        halves = []
        for part in (0, 1):
            z = jnp.concatenate(
                [
                    received[pl.ds(channel * 2 + part, 256, stride=8), :]
                    for channel in (2 * pair, 2 * pair + 1)
                ],
                axis=1,
            )
            zh, zl = split(z)
            rows = slice(128, 384) if part == 0 else slice(0, 256)
            halves.append(dot(w5[0, rows], zh) + dot(w5[0, rows], zl) + dot(w5[1, rows], zh))
        g[:, pair * 256 : pair * 256 + 256] = halves[0] + halves[1]
    low16 = (lax.broadcasted_iota(jnp.int32, (8, 128), 1) & 16) == 0

    def bins(channel, upper, tile_half):
        parts = []
        for part in (0, 1):
            blocks = []
            for low in range(4):
                at = part * 128 + low * 32 + upper * 16 + tile_half * 8
                blocks.append(g[at : at + 8, channel * 128 : channel * 128 + 128])
            parts.append(block_transpose(blocks))
        xr, xi = [parts[0][0]], [parts[1][0]]
        start = (middle + 2 * upper) * 16 + tile_half * 8
        for pulse in (1, 2, 3):
            tr = t5[pulse - 1, 0, start : start + 8, :]
            ti = t5[pulse - 1, 1, start : start + 8, :]
            r, i = parts[0][pulse], parts[1][pulse]
            xr.append(r * tr - i * ti)
            xi.append(r * ti + i * tr)
        ar, ai = xr[0] + xr[2], xi[0] + xi[2]
        br, bi = xr[0] - xr[2], xi[0] - xi[2]
        er, ei = xr[1] + xr[3], xi[1] + xi[3]
        dr, di = xr[1] - xr[3], xi[1] - xi[3]
        return [(ar + er, ai + ei), (br + di, bi - dr), (ar - er, ai - ei), (br - di, bi + dr)]

    for channel in range(4):
        for tile_half in range(2):
            values = [bins(channel, upper, tile_half) for upper in (0, 1)]
            for high in range(4):
                for part in (0, 1):
                    for upper in (0, 1):
                        at = high * 32 + upper * 16 + tile_half * 8
                        spectrum[channel, part, at : at + 8, :] = values[upper][high][part]
                    at = high * 16 + tile_half * 8
                    margin[channel, part, at : at + 8, :] = jnp.where(
                        low16, values[0][high][part], pltpu.roll(values[1][high][part], 16, 1)
                    )


def mixed(entries, values):
    real = imag = None
    for (mr, mi), (dr, di) in zip(entries, values):
        r = mr * dr - mi * di
        i = mr * di + mi * dr
        real = r if real is None else real + r
        imag = i if imag is None else imag + i
    return real, imag


def unfold_kernel(spectrum0, spectrum1, compact, unfolded, packed_mix, mix):
    group = lax.broadcasted_iota(jnp.int32, (256, 128), 1) & 96

    def expand(entry, carry):
        mix[entry] = lanes_taken(compact[...], group + entry)
        return carry

    lax.fori_loop(0, 32, expand, 0, unroll=EXPAND)
    low16 = (lax.broadcasted_iota(jnp.int32, (16, 128), 1) & 16) == 0

    def pack(entry, carry):
        for middle in range(2):
            for high in range(4):
                at = high * 64 + middle * 16
                packed_mix[entry, middle, high * 16 : high * 16 + 16, :] = jnp.where(
                    low16, mix[entry, at : at + 16, :], mix[entry, at + 32 : at + 48, :]
                )
        return carry

    lax.fori_loop(0, 32, pack, 0, unroll=2)

    def combine(upper, carry):
        for middle, spectrum in enumerate((spectrum0, spectrum1)):
            for high in range(4):
                for tile_half in range(2):
                    start = high * 32 + upper * 16 + tile_half * 8
                    rows = pl.ds(pl.multiple_of(start, 8), 8)
                    values = [(spectrum[c, 0, rows, :], spectrum[c, 1, rows, :]) for c in range(4)]
                    start = high * 64 + (middle + 2 * upper) * 16 + tile_half * 8
                    rows = pl.ds(pl.multiple_of(start, 8), 8)
                    for band in range(4):
                        entries = [
                            (mix[band * 4 + c, rows, :], mix[16 + band * 4 + c, rows, :])
                            for c in range(4)
                        ]
                        to = band * 64 + high * 16 + tile_half * 8
                        real, imag = mixed(entries, values)
                        unfolded[middle + 2 * upper, 0, to : to + 8, :] = real
                        unfolded[middle + 2 * upper, 1, to : to + 8, :] = imag
        return carry

    lax.fori_loop(0, 2, combine, 0)


def mul_i(value, quarter):
    r, i = value
    return [(r, i), (-i, r), (-r, -i), (i, -r)][quarter % 4]


def add(a, b):
    return (a[0] + b[0], a[1] + b[1])


def sub(a, b):
    return (a[0] - b[0], a[1] - b[1])


def inverse4(x):
    a, b = add(x[0], x[2]), sub(x[0], x[2])
    e, d = add(x[1], x[3]), mul_i(sub(x[1], x[3]), 1)
    return [add(a, e), add(b, d), sub(a, e), sub(b, d)]


def lanes_taken(value, index):
    return jnp.take_along_axis(value, index, axis=1)


def second_index(fh, fl, w6):
    def turned(a, b):
        return lax.dot_general(a, b, (((0,), (0,)), ((), ())), preferred_element_type=F32)

    total = None
    for part, columns in ((0, slice(256, 768)), (1, slice(0, 512))):
        rows = slice(part * 256, part * 256 + 256)
        value = (
            turned(fh[rows], w6[0, :, columns])
            + turned(fh[rows], w6[1, :, columns])
            + turned(fl[rows], w6[0, :, columns])
        )
        total = value if total is None else total + value
    return total


def first_index(y, t6, image, out, first_row, sem):
    copies = []
    for tile in range(2):
        at_row = slice(tile * 8, tile * 8 + 8)
        for column in range(2):
            inner = []
            for low in range(4):
                values = []
                for middle in range(4):
                    d1 = middle * 4 + low
                    at = low * 32 + middle // 2 * 16 + tile * 8
                    source = y[middle % 2]
                    r = source[at : at + 8, column * 128 : column * 128 + 128]
                    i = source[at : at + 8, 256 + column * 128 : 256 + column * 128 + 128]
                    if d1:
                        tr = t6[0, d1 : d1 + 1, column * 128 : column * 128 + 128]
                        ti = t6[1, d1 : d1 + 1, column * 128 : column * 128 + 128]
                        r, i = r * tr - i * ti, r * ti + i * tr
                    values.append((r, i))
                inner.append(inverse4(values))
            for qa in range(4):
                values = []
                for low in range(4):
                    v = inner[low][qa]
                    turn = low * qa
                    if turn % 4 == 0:
                        v = mul_i(v, turn // 4)
                    else:
                        c = math.cos(2 * math.pi * turn / 16)
                        s = math.sin(2 * math.pi * turn / 16)
                        v = (v[0] * c - v[1] * s, v[0] * s + v[1] * c)
                    values.append(v)
                for qb, v in enumerate(inverse4(values)):
                    lanes = (qa + 4 * qb) * 256 + column * 128
                    image[0, at_row, lanes : lanes + 128] = v[0]
                    image[1, at_row, lanes : lanes + 128] = v[1]
        for part in (0, 1):
            copy = pltpu.make_async_copy(
                image.at[part, at_row],
                out.at[part, first_row + tile * 8 : first_row + tile * 8 + 8],
                sem.at[tile * 2 + part],
            )
            copy.start()
            copies.append(copy)
    for copy in copies:
        copy.wait()


def tables(rate, half, mig, upper, middle, at):
    shape = (16, 128)
    lane = lax.broadcasted_iota(jnp.int32, shape, 1)
    row = lax.broadcasted_iota(jnp.int32, shape, 0)
    half_bit = lax.shift_right_logical(lane, 4) & 1
    width = jnp.broadcast_to(half[upper : upper + 1, :], shape)
    square = width * width
    inverse = 1.0 / square.astype(F32)
    moved = jnp.broadcast_to(mig[upper : upper + 1, :], shape)
    speed = jnp.broadcast_to(rate[upper : upper + 1, :], shape) * 16.0
    d = (row + at) * 16 + (half_bit * 2 + middle) * 4 + lax.shift_right_logical(lane, 5)
    centred = jnp.where(d >= 2048, d - 4096, d)
    c2 = centred * centred
    number = moved * jnp.minimum(c2, square) + lax.shift_right_logical(square, 1)
    shift = (number.astype(F32) * inverse).astype(jnp.int32)
    rest = number - shift * square
    shift = shift + jnp.where(rest >= square, 1, 0) - jnp.where(rest < 0, 1, 0)
    source = (lane & 15) + 16 * upper + shift
    turns = speed * (c2.astype(F32) * (1.0 / 4194304.0))
    turns = turns - jnp.floor(turns + 0.5)
    angle = turns * (2.0 * math.pi)
    inside = jnp.abs(centred) < width
    return source, jnp.where(inside, jnp.cos(angle), 0.0), jnp.where(inside, jnp.sin(angle), 0.0)


def lower_kernel(unfolded, rate, half, mig, w6, t6, out, kept, phase, index, fh, fl, y, image, sem):
    lane = lax.broadcasted_iota(jnp.int32, (16, 128), 1)
    second = (lane & 16) != 0
    for upper in (0, 1):
        for middle in range(2):
            for block in range(16):
                at = block * 16
                source, pr, pi = tables(rate, half, mig, upper, middle, at)
                lanes = (lane & 96) + (source & 31)
                values = []
                for part in (0, 1):
                    value = jnp.where(
                        second,
                        lanes_taken(unfolded[middle + 2, part, at : at + 16, :], lanes),
                        lanes_taken(unfolded[middle, part, at : at + 16, :], lanes),
                    )
                    if upper:
                        value = jnp.where(source >= 32, 0.0, value)
                    values.append(value)
                both = (values[0] * pr - values[1] * pi, values[0] * pi + values[1] * pr)
                if upper:
                    phase[middle, 0, at : at + 16, :] = jnp.where(source >= 32, pr, 0.0)
                    phase[middle, 1, at : at + 16, :] = jnp.where(source >= 32, pi, 0.0)
                    index[middle, at : at + 16, :] = (lane & 112) + (source & 15)
                for part, value in enumerate(both):
                    rows = slice(part * 256 + at, part * 256 + at + 16)
                    if upper:
                        kept[middle, rows, :] = value
                    else:
                        fh[middle, rows, :], fl[middle, rows, :] = split(value)
    for middle in range(2):
        y[middle] = second_index(fh.at[middle], fl.at[middle], w6)
    first_index((y.at[0], y.at[1]), t6, image, out, 0, sem)


def upper_half(middle, margin, packed_mix, kept, phase, index, w6, fh, fl):
    for high in range(4):
        rows = slice(high * 16, high * 16 + 16)
        values = [(margin[c, 0, rows, :], margin[c, 1, rows, :]) for c in range(4)]
        for band in range(4):
            entries = [
                (
                    packed_mix[band * 4 + c, middle, rows, :],
                    packed_mix[16 + band * 4 + c, middle, rows, :],
                )
                for c in range(4)
            ]
            at = band * 64 + high * 16
            lanes = index[middle, at : at + 16, :]
            r, i = [lanes_taken(value, lanes) for value in mixed(entries, values)]
            pr = phase[middle, 0, at : at + 16, :]
            pi = phase[middle, 1, at : at + 16, :]
            for part, value in enumerate((r * pr - i * pi, r * pi + i * pr)):
                to = slice(part * 256 + at, part * 256 + at + 16)
                fh[to, :], fl[to, :] = split(value + kept[middle, to, :])
    return second_index(fh, fl, w6)


def upper_first(margin, packed_mix, kept, phase, index, w6, y, fh, fl):
    y[...] = upper_half(0, margin, packed_mix, kept, phase, index, w6, fh, fl)


def upper_second(
    margin, packed_mix, kept, phase, index, w6, y, t6, _, out, fh, fl, z, image, sem
):
    z[...] = upper_half(1, margin, packed_mix, kept, phase, index, w6, fh, fl)
    first_index((y, z), t6, image, out, 16, sem)


VMEM = pl.BlockSpec(memory_space=pltpu.VMEM)
SMEM = pl.BlockSpec(memory_space=pltpu.SMEM)
HBM = pl.BlockSpec(memory_space=pltpu.HBM)
MIB = 1 << 20


def call(kernel, out_shape, scratch, flops, operands, in_specs=None, out_specs=VMEM, limit=8, **more):
    return pl.pallas_call(
        kernel,
        out_shape=out_shape,
        in_specs=in_specs or [VMEM] * len(operands),
        out_specs=out_specs,
        scratch_shapes=scratch,
        compiler_params=pltpu.CompilerParams(vmem_limit_bytes=limit * MIB),
        cost_estimate=pl.CostEstimate(flops=flops, bytes_accessed=2 * MIB, transcendentals=0),
        **more,
    )(*operands)


def shape(*dims, dtype=F32):
    return jax.ShapeDtypeStruct(dims, dtype)


def local(raw, chirp, reconstruction, delays, rate, half, mig):
    k = constants()
    raw = raw.reshape(16, 2, 64, 128).transpose(0, 2, 1, 3).reshape(16, 128, 128)
    chirp = chirp.reshape(2, 64, 128).transpose(1, 0, 2).reshape(128, 128)
    dma = pltpu.SemaphoreType.DMA
    compressed = call(
        range_kernel, shape(64, 4, 8, 128),
        [
            pltpu.VMEM((16, 128, 128), F32),
            pltpu.VMEM((128, 128), F32),
            pltpu.VMEM((2, 128, 384), BF16),
            pltpu.VMEM((4, 256, 256), BF16),
            pltpu.VMEM((2, 64, 128), F32),
            pltpu.VMEM((2048, 128), F32),
            dma((4,)),
            dma((16,)),
        ],
        1 << 30, (raw, chirp, k["wa"], k["wb"], k["t1"]), in_specs=[HBM] * 5, out_specs=HBM, limit=63,
    )
    received = lax.all_to_all(compressed.reshape(256, 8, 128), AXES, 0, 0, tiled=True)
    received = received.reshape(2048, 128)
    integers = shape(8, 128, dtype=jnp.int32)
    mix, rate, half, mig = call(
        mixing_kernel, (shape(256, 128), shape(8, 128), integers, integers),
        [pltpu.VMEM((32, 1024), F32), pltpu.VMEM((1024, 32), F32)],
        1 << 24,
        (delays, reconstruction, rate.reshape(1, 32), half.reshape(1, 32), mig.reshape(1, 32)),
        in_specs=[SMEM] + [VMEM] * 4, out_specs=(VMEM,) * 4,
    )
    pairs = [(i, i - 1) for i in range(1, lax.axis_size(AXES))]
    spectra, margins = [], []
    for middle in range(2):
        spectrum, margin = call(
            functools.partial(azimuth_kernel, middle),
            (shape(4, 2, 128, 128), shape(4, 2, 64, 128)), [pltpu.VMEM((256, 512), F32)],
            1 << 29, (received, k[f"w5{middle}"], k["t5"]), out_specs=(VMEM,) * 2,
        )
        spectra.append(spectrum)
        margins.append(lax.ppermute(margin, AXES, pairs))
    unfolded, packed_mix = call(
        unfold_kernel, (shape(4, 2, 256, 128), shape(32, 2, 64, 128)),
        [pltpu.VMEM((32, 256, 128), F32)],
        1 << 30, (*spectra, mix), out_specs=(VMEM, VMEM), limit=12,
    )
    halves = [pltpu.VMEM((2, 512, 128), BF16)] * 2
    image, kept, phase, index = call(
        lower_kernel,
        (
            shape(2, 32, 4096),
            shape(2, 512, 128),
            shape(2, 2, 256, 128),
            shape(2, 256, 128, dtype=jnp.int32),
        ),
        halves + [pltpu.VMEM((2, 128, 512), F32), pltpu.VMEM((2, 16, 4096), F32), dma((4,))],
        1 << 30, (unfolded, rate, half, mig, k["w6"], k["t6"]), out_specs=(HBM, VMEM, VMEM, VMEM),
    )
    halves = [pltpu.VMEM((512, 128), BF16)] * 2
    y = call(
        upper_first, shape(128, 512), halves, 1 << 30,
        (margins[0], packed_mix, kept, phase, index, k["w6"]),
    )
    return call(
        upper_second, shape(2, 32, 4096),
        halves + [pltpu.VMEM((128, 512), F32), pltpu.VMEM((2, 16, 4096), F32), dma((4,))],
        1 << 30, (margins[1], packed_mix, kept, phase, index, k["w6"], y, k["t6"], image),
        in_specs=[VMEM] * 8 + [HBM], out_specs=HBM, input_output_aliases={8: 0},
    )


def solution(mesh):
    in_specs = (P(AXES, None, None, None), P(), P(), P(), P(AXES), P(AXES), P(AXES))
    return jax.shard_map(
        local, mesh=mesh, in_specs=in_specs, out_specs=P(None, AXES, None), check_vma=False
    )
```

```python
import functools
import math

import jax
import jax.numpy as jnp
import ml_dtypes
import numpy as np
from jax import lax
from jax.experimental import pallas as pl
from jax.experimental.pallas import tpu as pltpu
from jax.sharding import PartitionSpec as P

AXES = ("az", "rg")
GROUPS = 2
EXPAND = 8
F32 = jnp.float32
BF16 = jnp.bfloat16


def split_np(matrix):
    matrix = np.asarray(matrix, np.float64)
    high = matrix.astype(np.float32).astype(ml_dtypes.bfloat16)
    low = (matrix - high.astype(np.float64)).astype(np.float32).astype(ml_dtypes.bfloat16)
    return high, low


def phases(rows, columns, length, sign):
    turns = np.outer(np.asarray(rows), np.asarray(columns)) % length
    angle = sign * 2.0 * np.pi * turns / length
    return np.cos(angle), np.sin(angle)


def complex_left(cosine, sine):
    return np.block([[cosine, -sine], [sine, cosine]])


@functools.lru_cache(None)
def constants():
    out = {}
    c, s = phases(np.arange(64), np.arange(64), 64, -1)
    m = complex_left(c, s).reshape(128, 2, 64).transpose(0, 2, 1).reshape(128, 128)
    h, l = split_np(m)
    first = np.concatenate([h, h, l], axis=1)
    c, s = phases(np.arange(64), np.arange(64), 64, 1)
    m = complex_left(c, s).reshape(2, 2, 32, 128).transpose(1, 0, 2, 3).reshape(128, 128)
    h, l = split_np(m / 8192.0)
    out["wa"] = np.stack([first, np.concatenate([h, h, l], axis=1)])
    order = np.arange(128).reshape(64, 2).T.reshape(-1)
    c, s = phases(np.arange(128), order, 128, -1)
    pair = split_np(np.block([[c, s], [-s, c]]))
    c, s = phases(order, np.arange(128), 128, 1)
    out["wb"] = np.stack(pair + split_np(np.block([[c, s], [-s, c]])))
    c, s = phases(np.arange(64), np.arange(128), 8192, -1)
    out["t1"] = np.stack([c, s]).astype(np.float32)
    fm = np.arange(256).reshape(16, 4, 4).transpose(2, 1, 0)
    sets = []
    for middle in range(2):
        c, s = phases(fm[:, middle::2].reshape(-1), np.arange(256), 256, 1)
        sets.append(np.concatenate([s, c, -s], axis=0) / 32.0)
    for middle in range(2):
        out[f"w5{middle}"] = np.stack(split_np(sets[middle]))
    fm = fm.reshape(-1)
    grid = fm.reshape(4, 64)
    tables = []
    for pulse in (1, 2, 3):
        angle = -2.0 * np.pi * (pulse * grid % 1024) / 1024
        angle = np.repeat(angle.T, 32, axis=1)
        tables.append(np.stack([np.cos(angle), np.sin(angle)]))
    out["t5"] = np.stack(tables).astype(np.float32)
    c, s = phases(np.arange(256), np.arange(256), 256, 1)
    out["w6"] = np.stack(split_np(np.concatenate([-s, c, s], axis=1) / 64.0))
    c, s = phases(np.arange(16), np.arange(256), 4096, 1)
    out["t6"] = np.stack([c, s]).astype(np.float32)
    return out


def split(value):
    high = value.astype(BF16)
    return high, (value - high.astype(F32)).astype(BF16)


def dot(a, b):
    return jnp.dot(a, b, preferred_element_type=F32)


def dot3(a, bh, bl):
    ah, al = split(a)
    return dot(ah, bh) + dot(ah, bl) + dot(al, bh)


def in_groups(rows, high, low, groups=GROUPS):
    size = len(rows) // groups
    out = []
    for group in range(groups):
        value = dot3(jnp.concatenate(rows[group * size : group * size + size], axis=0), high, low)
        height = rows[0].shape[0]
        out += [value[n * height : n * height + height] for n in range(size)]
    return out


def block_transpose(v):
    lane = lax.broadcasted_iota(jnp.int32, v[0].shape, 1)
    low64 = lane < 64
    low32 = (lane & 32) == 0
    a = [None] * 4
    for i in (0, 1):
        a[i] = jnp.where(low64, v[i], pltpu.roll(v[i + 2], 64, 1))
        a[i + 2] = jnp.where(low64, pltpu.roll(v[i], 64, 1), v[i + 2])
    o = [None] * 4
    for i in (0, 2):
        o[i] = jnp.where(low32, a[i], pltpu.roll(a[i + 1], 32, 1))
        o[i + 1] = jnp.where(low32, pltpu.roll(a[i], 96, 1), a[i + 1])
    return o


def range_kernel(raw_hbm, chirp_hbm, wa_hbm, wb_hbm, t1_hbm, out, raw, chirp, wa, wb, t1, turned_out, sem, raw_sem, out_sem):
    copies = [
        pltpu.make_async_copy(source, target, sem.at[n])
        for n, (source, target) in enumerate(
            ((wa_hbm, wa), (t1_hbm, t1), (chirp_hbm, chirp), (wb_hbm, wb))
        )
    ]
    echoes = [
        [
            pltpu.make_async_copy(
                raw_hbm.at[p * 4 + channel], raw.at[p * 4 + channel], raw_sem.at[p * 4 + channel]
            )
            for p in range(4)
        ]
        for channel in range(4)
    ]
    copies[0].start()
    for channel in range(4):
        for copy in echoes[channel]:
            copy.start()
    for copy in copies[1:]:
        copy.start()
    copies[0].wait()
    for channel in range(4):
        for copy in echoes[channel]:
            copy.wait()
    spectra = []
    for channel in range(4):
        x = jnp.concatenate([raw[pulse * 4 + channel] for pulse in range(4)], axis=1)
        xh, xl = split(x)
        spectra.append(dot(wa[0], jnp.concatenate([xh, xl, xh], axis=0)))
    for copy in copies[1:]:
        copy.wait()
    tr, ti = t1[0], t1[1]
    chirp_parts = []
    for part in (0, 1):
        natural = chirp[pl.ds(part, 64, stride=2), :]
        turned = natural.T
        chirp_parts.append(jnp.concatenate([turned[:64], turned[64:]], axis=1))
    cr, ci = chirp_parts
    rows = []
    for a in spectra:
        for pulse in range(4):
            ar = a[:64, pulse * 128 : pulse * 128 + 128]
            ai = a[64:, pulse * 128 : pulse * 128 + 128]
            rows.append(jnp.concatenate([ar * tr - ai * ti, ar * ti + ai * tr], axis=1))
    b = in_groups(rows, wb[0], wb[1])
    rows = []
    for row in range(16):
        br, bi = b[row][:, :128], b[row][:, 128:]
        rows.append(jnp.concatenate([br * cr + bi * ci, bi * cr - br * ci], axis=1))
    b = in_groups(rows, wb[2], wb[3])
    stacked = []
    for channel in range(4):
        columns = []
        for row in range(channel * 4, channel * 4 + 4):
            br, bi = b[row][:, :128], b[row][:, 128:]
            columns.append(jnp.concatenate([br * tr + bi * ti, bi * tr - br * ti], axis=0))
        xh, xl = split(jnp.concatenate(columns, axis=1))
        stacked.append(jnp.concatenate([xh, xl, xh], axis=0))
    results = []
    for half in range(2):
        for channel in range(4):
            a = dot(wa[1, half * 64 : half * 64 + 64], stacked[channel])
            for part in (0, 1):
                o = block_transpose(
                    [a[part * 32 : part * 32 + 32, p * 128 : p * 128 + 128] for p in range(4)]
                )
                for low in range(4):
                    at = low * 512 + half * 256 + channel * 2 + part
                    turned_out[pl.ds(at, 32, stride=8), :] = o[low]
        for low in range(4):
            copy = pltpu.make_async_copy(
                turned_out.at[pl.ds(low * 512 + half * 256, 256)].reshape(32, 8, 128),
                out.at[pl.ds(half * 32, 32), low],
                out_sem.at[half * 4 + low],
            )
            copy.start()
            results.append(copy)
    for copy in results:
        copy.wait()


def packed(value):
    whole = jnp.concatenate([jnp.broadcast_to(value[...], (8, 32))] * 4, axis=1)
    lane = lax.broadcasted_iota(jnp.int32, (8, 128), 1)
    row = lax.broadcasted_iota(jnp.int32, (8, 128), 0)
    return lanes_taken(whole, (lane & 15) + 16 * (row & 1))


def mixing_kernel(
    delays, reconstruction, rate, half, mig, mix, rate_out, half_out, mig_out, flat, turned
):
    rate_out[...] = packed(rate)
    half_out[...] = packed(half)
    mig_out[...] = packed(mig)
    channel = lax.broadcasted_iota(jnp.int32, (4, 1024), 0)
    frequency = lax.broadcasted_iota(jnp.int32, (4, 1024), 1)
    delay = jnp.where(
        channel < 2,
        jnp.where(channel < 1, delays[0], delays[1]),
        jnp.where(channel < 3, delays[2], delays[3]),
    )
    angle = (2.0 * math.pi / 1024) * ((frequency * delay) & 1023).astype(F32)
    cosine, sine = jnp.cos(angle), jnp.sin(angle)
    for band in range(4):
        real, imag = reconstruction[0, band], reconstruction[1, band]
        flat[band * 4 : band * 4 + 4, :] = real * cosine - imag * sine
        flat[16 + band * 4 : 16 + band * 4 + 4, :] = real * sine + imag * cosine
    for block in range(8):
        turned[block * 128 : block * 128 + 128, :] = flat[:, block * 128 : block * 128 + 128].T
    for high in range(4):
        for middle in range(4):
            pieces = [
                turned[pl.ds(high * 256 + middle * 4 + low, 16, stride=16), :] for low in range(4)
            ]
            at = high * 64 + middle * 16
            mix[at : at + 16, :] = jnp.concatenate(pieces, axis=1)


def azimuth_kernel(middle, received, w5, t5, spectrum, margin, g):
    for pair in range(2):
        halves = []
        for part in (0, 1):
            z = jnp.concatenate(
                [
                    received[pl.ds(channel * 2 + part, 256, stride=8), :]
                    for channel in (2 * pair, 2 * pair + 1)
                ],
                axis=1,
            )
            zh, zl = split(z)
            rows = slice(128, 384) if part == 0 else slice(0, 256)
            halves.append(dot(w5[0, rows], zh) + dot(w5[0, rows], zl) + dot(w5[1, rows], zh))
        g[:, pair * 256 : pair * 256 + 256] = halves[0] + halves[1]
    low16 = (lax.broadcasted_iota(jnp.int32, (8, 128), 1) & 16) == 0

    def bins(channel, upper, tile_half):
        parts = []
        for part in (0, 1):
            blocks = []
            for low in range(4):
                at = part * 128 + low * 32 + upper * 16 + tile_half * 8
                blocks.append(g[at : at + 8, channel * 128 : channel * 128 + 128])
            parts.append(block_transpose(blocks))
        xr, xi = [parts[0][0]], [parts[1][0]]
        start = (middle + 2 * upper) * 16 + tile_half * 8
        for pulse in (1, 2, 3):
            tr = t5[pulse - 1, 0, start : start + 8, :]
            ti = t5[pulse - 1, 1, start : start + 8, :]
            r, i = parts[0][pulse], parts[1][pulse]
            xr.append(r * tr - i * ti)
            xi.append(r * ti + i * tr)
        ar, ai = xr[0] + xr[2], xi[0] + xi[2]
        br, bi = xr[0] - xr[2], xi[0] - xi[2]
        er, ei = xr[1] + xr[3], xi[1] + xi[3]
        dr, di = xr[1] - xr[3], xi[1] - xi[3]
        return [(ar + er, ai + ei), (br + di, bi - dr), (ar - er, ai - ei), (br - di, bi + dr)]

    for channel in range(4):
        for tile_half in range(2):
            values = [bins(channel, upper, tile_half) for upper in (0, 1)]
            for high in range(4):
                for part in (0, 1):
                    for upper in (0, 1):
                        at = high * 32 + upper * 16 + tile_half * 8
                        spectrum[channel, part, at : at + 8, :] = values[upper][high][part]
                    at = high * 16 + tile_half * 8
                    margin[channel, part, at : at + 8, :] = jnp.where(
                        low16, values[0][high][part], pltpu.roll(values[1][high][part], 16, 1)
                    )


def mixed(entries, values):
    real = imag = None
    for (mr, mi), (dr, di) in zip(entries, values):
        r = mr * dr - mi * di
        i = mr * di + mi * dr
        real = r if real is None else real + r
        imag = i if imag is None else imag + i
    return real, imag


def unfold_kernel(spectrum0, spectrum1, compact, unfolded, packed_mix, mix):
    group = lax.broadcasted_iota(jnp.int32, (256, 128), 1) & 96

    def expand(entry, carry):
        mix[entry] = lanes_taken(compact[...], group + entry)
        return carry

    lax.fori_loop(0, 32, expand, 0, unroll=EXPAND)
    low16 = (lax.broadcasted_iota(jnp.int32, (16, 128), 1) & 16) == 0

    def pack(entry, carry):
        for middle in range(2):
            for high in range(4):
                at = high * 64 + middle * 16
                packed_mix[entry, middle, high * 16 : high * 16 + 16, :] = jnp.where(
                    low16, mix[entry, at : at + 16, :], mix[entry, at + 32 : at + 48, :]
                )
        return carry

    lax.fori_loop(0, 32, pack, 0, unroll=2)

    def combine(upper, carry):
        for middle, spectrum in enumerate((spectrum0, spectrum1)):
            for high in range(4):
                for tile_half in range(2):
                    start = high * 32 + upper * 16 + tile_half * 8
                    rows = pl.ds(pl.multiple_of(start, 8), 8)
                    values = [(spectrum[c, 0, rows, :], spectrum[c, 1, rows, :]) for c in range(4)]
                    start = high * 64 + (middle + 2 * upper) * 16 + tile_half * 8
                    rows = pl.ds(pl.multiple_of(start, 8), 8)
                    for band in range(4):
                        entries = [
                            (mix[band * 4 + c, rows, :], mix[16 + band * 4 + c, rows, :])
                            for c in range(4)
                        ]
                        to = band * 64 + high * 16 + tile_half * 8
                        real, imag = mixed(entries, values)
                        unfolded[middle + 2 * upper, 0, to : to + 8, :] = real
                        unfolded[middle + 2 * upper, 1, to : to + 8, :] = imag
        return carry

    lax.fori_loop(0, 2, combine, 0)


def mul_i(value, quarter):
    r, i = value
    return [(r, i), (-i, r), (-r, -i), (i, -r)][quarter % 4]


def add(a, b):
    return (a[0] + b[0], a[1] + b[1])


def sub(a, b):
    return (a[0] - b[0], a[1] - b[1])


def inverse4(x):
    a, b = add(x[0], x[2]), sub(x[0], x[2])
    e, d = add(x[1], x[3]), mul_i(sub(x[1], x[3]), 1)
    return [add(a, e), add(b, d), sub(a, e), sub(b, d)]


def lanes_taken(value, index):
    return jnp.take_along_axis(value, index, axis=1)


def second_index(fh, fl, w6):
    def turned(a, b):
        return lax.dot_general(a, b, (((0,), (0,)), ((), ())), preferred_element_type=F32)

    total = None
    for part, columns in ((0, slice(256, 768)), (1, slice(0, 512))):
        rows = slice(part * 256, part * 256 + 256)
        value = (
            turned(fh[rows], w6[0, :, columns])
            + turned(fh[rows], w6[1, :, columns])
            + turned(fl[rows], w6[0, :, columns])
        )
        total = value if total is None else total + value
    return total


def first_index(y, t6, image, out, first_row, sem):
    copies = []
    for tile in range(2):
        at_row = slice(tile * 8, tile * 8 + 8)
        for column in range(2):
            inner = []
            for low in range(4):
                values = []
                for middle in range(4):
                    d1 = middle * 4 + low
                    at = low * 32 + middle // 2 * 16 + tile * 8
                    source = y[middle % 2]
                    r = source[at : at + 8, column * 128 : column * 128 + 128]
                    i = source[at : at + 8, 256 + column * 128 : 256 + column * 128 + 128]
                    if d1:
                        tr = t6[0, d1 : d1 + 1, column * 128 : column * 128 + 128]
                        ti = t6[1, d1 : d1 + 1, column * 128 : column * 128 + 128]
                        r, i = r * tr - i * ti, r * ti + i * tr
                    values.append((r, i))
                inner.append(inverse4(values))
            for qa in range(4):
                values = []
                for low in range(4):
                    v = inner[low][qa]
                    turn = low * qa
                    if turn % 4 == 0:
                        v = mul_i(v, turn // 4)
                    else:
                        c = math.cos(2 * math.pi * turn / 16)
                        s = math.sin(2 * math.pi * turn / 16)
                        v = (v[0] * c - v[1] * s, v[0] * s + v[1] * c)
                    values.append(v)
                for qb, v in enumerate(inverse4(values)):
                    lanes = (qa + 4 * qb) * 256 + column * 128
                    image[0, at_row, lanes : lanes + 128] = v[0]
                    image[1, at_row, lanes : lanes + 128] = v[1]
        for part in (0, 1):
            copy = pltpu.make_async_copy(
                image.at[part, at_row],
                out.at[part, first_row + tile * 8 : first_row + tile * 8 + 8],
                sem.at[tile * 2 + part],
            )
            copy.start()
            copies.append(copy)
    for copy in copies:
        copy.wait()


def tables(rate, half, mig, upper, middle, at):
    shape = (16, 128)
    lane = lax.broadcasted_iota(jnp.int32, shape, 1)
    row = lax.broadcasted_iota(jnp.int32, shape, 0)
    half_bit = lax.shift_right_logical(lane, 4) & 1
    width = jnp.broadcast_to(half[upper : upper + 1, :], shape)
    square = width * width
    inverse = 1.0 / square.astype(F32)
    moved = jnp.broadcast_to(mig[upper : upper + 1, :], shape)
    speed = jnp.broadcast_to(rate[upper : upper + 1, :], shape) * 16.0
    d = (row + at) * 16 + (half_bit * 2 + middle) * 4 + lax.shift_right_logical(lane, 5)
    centred = jnp.where(d >= 2048, d - 4096, d)
    c2 = centred * centred
    number = moved * jnp.minimum(c2, square) + lax.shift_right_logical(square, 1)
    shift = (number.astype(F32) * inverse).astype(jnp.int32)
    rest = number - shift * square
    shift = shift + jnp.where(rest >= square, 1, 0) - jnp.where(rest < 0, 1, 0)
    source = (lane & 15) + 16 * upper + shift
    turns = speed * (c2.astype(F32) * (1.0 / 4194304.0))
    turns = turns - jnp.floor(turns + 0.5)
    angle = turns * (2.0 * math.pi)
    inside = jnp.abs(centred) < width
    return source, jnp.where(inside, jnp.cos(angle), 0.0), jnp.where(inside, jnp.sin(angle), 0.0)


def lower_kernel(unfolded, rate, half, mig, w6, t6, out, kept, phase, index, fh, fl, y, image, sem):
    lane = lax.broadcasted_iota(jnp.int32, (16, 128), 1)
    second = (lane & 16) != 0
    for upper in (0, 1):
        for middle in range(2):
            for block in range(16):
                at = block * 16
                source, pr, pi = tables(rate, half, mig, upper, middle, at)
                lanes = (lane & 96) + (source & 31)
                values = []
                for part in (0, 1):
                    value = jnp.where(
                        second,
                        lanes_taken(unfolded[middle + 2, part, at : at + 16, :], lanes),
                        lanes_taken(unfolded[middle, part, at : at + 16, :], lanes),
                    )
                    if upper:
                        value = jnp.where(source >= 32, 0.0, value)
                    values.append(value)
                both = (values[0] * pr - values[1] * pi, values[0] * pi + values[1] * pr)
                if upper:
                    phase[middle, 0, at : at + 16, :] = jnp.where(source >= 32, pr, 0.0)
                    phase[middle, 1, at : at + 16, :] = jnp.where(source >= 32, pi, 0.0)
                    index[middle, at : at + 16, :] = (lane & 112) + (source & 15)
                for part, value in enumerate(both):
                    rows = slice(part * 256 + at, part * 256 + at + 16)
                    if upper:
                        kept[middle, rows, :] = value
                    else:
                        fh[middle, rows, :], fl[middle, rows, :] = split(value)
    for middle in range(2):
        y[middle] = second_index(fh.at[middle], fl.at[middle], w6)
    first_index((y.at[0], y.at[1]), t6, image, out, 0, sem)


def upper_half(middle, margin, packed_mix, kept, phase, index, w6, fh, fl):
    for high in range(4):
        rows = slice(high * 16, high * 16 + 16)
        values = [(margin[c, 0, rows, :], margin[c, 1, rows, :]) for c in range(4)]
        for band in range(4):
            entries = [
                (
                    packed_mix[band * 4 + c, middle, rows, :],
                    packed_mix[16 + band * 4 + c, middle, rows, :],
                )
                for c in range(4)
            ]
            at = band * 64 + high * 16
            lanes = index[middle, at : at + 16, :]
            r, i = [lanes_taken(value, lanes) for value in mixed(entries, values)]
            pr = phase[middle, 0, at : at + 16, :]
            pi = phase[middle, 1, at : at + 16, :]
            for part, value in enumerate((r * pr - i * pi, r * pi + i * pr)):
                to = slice(part * 256 + at, part * 256 + at + 16)
                fh[to, :], fl[to, :] = split(value + kept[middle, to, :])
    return second_index(fh, fl, w6)


def upper_first(margin, packed_mix, kept, phase, index, w6, y, fh, fl):
    y[...] = upper_half(0, margin, packed_mix, kept, phase, index, w6, fh, fl)


def upper_second(
    margin, packed_mix, kept, phase, index, w6, y, t6, _, out, fh, fl, z, image, sem
):
    z[...] = upper_half(1, margin, packed_mix, kept, phase, index, w6, fh, fl)
    first_index((y, z), t6, image, out, 16, sem)


VMEM = pl.BlockSpec(memory_space=pltpu.VMEM)
SMEM = pl.BlockSpec(memory_space=pltpu.SMEM)
HBM = pl.BlockSpec(memory_space=pltpu.HBM)
MIB = 1 << 20


def call(kernel, out_shape, scratch, flops, operands, in_specs=None, out_specs=VMEM, limit=8, **more):
    return pl.pallas_call(
        kernel,
        out_shape=out_shape,
        in_specs=in_specs or [VMEM] * len(operands),
        out_specs=out_specs,
        scratch_shapes=scratch,
        compiler_params=pltpu.CompilerParams(vmem_limit_bytes=limit * MIB),
        cost_estimate=pl.CostEstimate(flops=flops, bytes_accessed=2 * MIB, transcendentals=0),
        **more,
    )(*operands)


def shape(*dims, dtype=F32):
    return jax.ShapeDtypeStruct(dims, dtype)


def local(raw, chirp, reconstruction, delays, rate, half, mig):
    k = constants()
    raw = raw.reshape(16, 2, 64, 128).transpose(0, 2, 1, 3).reshape(16, 128, 128)
    chirp = chirp.reshape(2, 64, 128).transpose(1, 0, 2).reshape(128, 128)
    dma = pltpu.SemaphoreType.DMA
    compressed = call(
        range_kernel, shape(64, 4, 8, 128),
        [
            pltpu.VMEM((16, 128, 128), F32),
            pltpu.VMEM((128, 128), F32),
            pltpu.VMEM((2, 128, 384), BF16),
            pltpu.VMEM((4, 256, 256), BF16),
            pltpu.VMEM((2, 64, 128), F32),
            pltpu.VMEM((2048, 128), F32),
            dma((4,)),
            dma((16,)),
            dma((8,)),
        ],
        1 << 30, (raw, chirp, k["wa"], k["wb"], k["t1"]), in_specs=[HBM] * 5, out_specs=HBM, limit=63,
    )
    received = lax.all_to_all(compressed.reshape(256, 8, 128), AXES, 0, 0, tiled=True)
    received = received.reshape(2048, 128)
    integers = shape(8, 128, dtype=jnp.int32)
    mix, rate, half, mig = call(
        mixing_kernel, (shape(256, 128), shape(8, 128), integers, integers),
        [pltpu.VMEM((32, 1024), F32), pltpu.VMEM((1024, 32), F32)],
        1 << 24,
        (delays, reconstruction, rate.reshape(1, 32), half.reshape(1, 32), mig.reshape(1, 32)),
        in_specs=[SMEM] + [VMEM] * 4, out_specs=(VMEM,) * 4,
    )
    pairs = [(i, i - 1) for i in range(1, lax.axis_size(AXES))]
    spectra, margins = [], []
    for middle in range(2):
        spectrum, margin = call(
            functools.partial(azimuth_kernel, middle),
            (shape(4, 2, 128, 128), shape(4, 2, 64, 128)), [pltpu.VMEM((256, 512), F32)],
            1 << 29, (received, k[f"w5{middle}"], k["t5"]), out_specs=(VMEM,) * 2,
        )
        spectra.append(spectrum)
        margins.append(lax.ppermute(margin, AXES, pairs))
    unfolded, packed_mix = call(
        unfold_kernel, (shape(4, 2, 256, 128), shape(32, 2, 64, 128)),
        [pltpu.VMEM((32, 256, 128), F32)],
        1 << 30, (*spectra, mix), out_specs=(VMEM, VMEM), limit=12,
    )
    halves = [pltpu.VMEM((2, 512, 128), BF16)] * 2
    image, kept, phase, index = call(
        lower_kernel,
        (
            shape(2, 32, 4096),
            shape(2, 512, 128),
            shape(2, 2, 256, 128),
            shape(2, 256, 128, dtype=jnp.int32),
        ),
        halves + [pltpu.VMEM((2, 128, 512), F32), pltpu.VMEM((2, 16, 4096), F32), dma((4,))],
        1 << 30, (unfolded, rate, half, mig, k["w6"], k["t6"]), out_specs=(HBM, VMEM, VMEM, VMEM),
    )
    halves = [pltpu.VMEM((512, 128), BF16)] * 2
    y = call(
        upper_first, shape(128, 512), halves, 1 << 30,
        (margins[0], packed_mix, kept, phase, index, k["w6"]),
    )
    return call(
        upper_second, shape(2, 32, 4096),
        halves + [pltpu.VMEM((128, 512), F32), pltpu.VMEM((2, 16, 4096), F32), dma((4,))],
        1 << 30, (margins[1], packed_mix, kept, phase, index, k["w6"], y, k["t6"], image),
        in_specs=[VMEM] * 8 + [HBM], out_specs=HBM, input_output_aliases={8: 0},
    )


def solution(mesh):
    in_specs = (P(AXES, None, None, None), P(), P(), P(), P(AXES), P(AXES), P(AXES))
    return jax.shard_map(
        local, mesh=mesh, in_specs=in_specs, out_specs=P(None, AXES, None), check_vma=False
    )
```
